256 devices in a mesh: ctx: 32 (over z, x), grp: 8 (over y, core).
Axes of the slice: x: 4, y: 4, z: 8, core: 2. Of those that a mesh axis runs over, the one named last changes fastest.
Arguments:
- queries: bfloat16 [262144, 512], P(('grp', 'ctx')), parts along dimension 0, may hold values from -6 to 6
- key_vectors: bfloat16 [262144, 512], P(('grp', 'ctx')), parts along dimension 0, may hold values from -6 to 6
- value_rows: bfloat16 [262144, 512], P(('grp', 'ctx')), parts along dimension 0, may hold values from -6 to 6
- cotangent: bfloat16 [262144, 512], P(('grp', 'ctx')), parts along dimension 0, may hold values from -6 to 6
Outputs:
- attended: bfloat16 [262144, 512], P(('grp', 'ctx')), parts along dimension 0
- grad_queries: bfloat16 [262144, 512], P(('grp', 'ctx')), parts along dimension 0
- grad_keys: bfloat16 [262144, 512], P(('grp', 'ctx')), parts along dimension 0
- grad_values: bfloat16 [262144, 512], P(('grp', 'ctx')), parts along dimension 0
The draws below stay inside these ranges and needn't reach their ends.
There are 8 independent parts, one for each index of `grp`. The reference program is written for one: setup_inputs(seed, part) draws one part's arguments, and reference() takes and returns one part's arrays. A program takes and returns all parts, laid end to end along the dimension named above; each array names one. Nothing has to cross between parts.
All inputs are finite; a program needn't handle non-finite values.
Results may differ from the reference program's by a relative error of at most 0.0025.
Values sent between devices are 32-bit elements; how exact they have to be, the bound alone decides.
A program may use at most 128 MiB of HBM per device.

```python
import math
import jax
import jax.numpy as jnp
from jax import lax

DH = 128
HEADS = 4
L_DEV = 1024
SEQ = 32768
COLS = 512


def steps_of(rng, extent, shards, low, largest):
    gain, own = 1.0, jax.random.fold_in(rng, 6)
    for axis_at, blocks in shards:
        draws = jnp.exp(jax.random.uniform(jax.random.fold_in(own, axis_at), (blocks,), jnp.float32, low / len(shards), largest / len(shards)))
        gain = gain * jnp.repeat(draws, extent[axis_at] // blocks).reshape([-1 if axis == axis_at else 1 for axis in range(len(extent))])
    return gain


def gaussian(own_key, shape, scale, bound, shards=(), kind=jnp.bfloat16):
    level = steps_of(own_key, shape, shards, -0.22, 0.18) if shards else 1.0
    values = jax.random.normal(own_key, shape, jnp.float32) * scale * level
    return jnp.minimum(jnp.maximum(values, -bound), bound).astype(kind)


def setup_inputs(seed: int = 0, part: int = 0) -> dict:
    arg_keys = jax.random.split(jax.random.key(seed), 5)
    own_keys = jax.random.split(jax.random.fold_in(arg_keys[4], part), 5)
    queries = gaussian(own_keys[0], (SEQ, COLS), 1.0, 6.0, ((0, 32),))
    key_vectors = gaussian(own_keys[1], (SEQ, COLS), 1.0, 6.0, ((0, 32),))
    value_rows = gaussian(own_keys[2], (SEQ, COLS), 1.0, 6.0, ((0, 32),))
    cotangent = gaussian(own_keys[3], (SEQ, COLS), 1.0, 6.0, ((0, 32),))
    return dict(queries=queries, key_vectors=key_vectors, value_rows=value_rows, cotangent=cotangent)


def inner_first(left, right):
    return lax.dot_general(left, right, (((0,), (0,)), ((), ())), preferred_element_type=jnp.float32)

def inner_last(left, right):
    return lax.dot_general(left, right, (((1,), (1,)), ((), ())), preferred_element_type=jnp.float32)

def split_state(state):
    upper = lax.optimization_barrier(state.astype(jnp.bfloat16))
    lower = (state - upper.astype(jnp.float32)).astype(jnp.bfloat16)
    return (upper, lower)

def block_states(blocks):
    queries, key_vectors, value_rows, cotangent = blocks
    width = DH
    states = []
    grads = []
    for head_index in range(HEADS):
        cols = slice(head_index * width, (head_index + 1) * width)
        states.append(inner_first(key_vectors[:, cols], value_rows[:, cols]))
        grads.append(inner_first(queries[:, cols], cotangent[:, cols]))
    return (jnp.stack(states), jnp.stack(grads))

def block_outputs(queries, key_vectors, value_rows, cotangent, prefix_state, suffix_grad, factor):
    width = DH
    length = queries.shape[0]
    causal = lax.broadcasted_iota(jnp.int32, (length, length), 0) >= lax.broadcasted_iota(jnp.int32, (length, length), 1)
    results = ([], [], [], [])
    prefix_hi, prefix_lo = split_state(prefix_state)
    suffix_hi, suffix_lo = split_state(suffix_grad)
    for head_index in range(HEADS):
        cols = slice(head_index * width, (head_index + 1) * width)
        query_head = queries[:, cols]
        key_head = key_vectors[:, cols]
        value_head = value_rows[:, cols]
        cot_head = cotangent[:, cols]
        state_hi = prefix_hi[head_index]
        state_lo = prefix_lo[head_index]
        grad_hi = suffix_hi[head_index]
        grad_lo = suffix_lo[head_index]
        weights = jnp.where(causal, inner_last(query_head, key_head), 0.0).astype(jnp.bfloat16)
        back_weights = jnp.where(causal, inner_last(cot_head, value_head), 0.0).astype(jnp.bfloat16)
        attended = jnp.dot(weights, value_head, preferred_element_type=jnp.float32) + jnp.dot(query_head, state_hi, preferred_element_type=jnp.float32) + jnp.dot(query_head, state_lo, preferred_element_type=jnp.float32)
        grad_q = jnp.dot(back_weights, key_head, preferred_element_type=jnp.float32) + inner_last(cot_head, state_hi) + inner_last(cot_head, state_lo)
        grad_k = inner_first(back_weights, query_head) + inner_last(value_head, grad_hi) + inner_last(value_head, grad_lo)
        grad_v = inner_first(weights, cot_head) + jnp.dot(key_head, grad_hi, preferred_element_type=jnp.float32) + jnp.dot(key_head, grad_lo, preferred_element_type=jnp.float32)
        for target, source in zip(results, (attended, grad_q, grad_k, grad_v)):
            target.append((factor * source).astype(jnp.bfloat16))
    return tuple((jnp.concatenate(parts, axis=1) for parts in results))

def adding(running, increment):
    return (running + increment, running)

def reference(queries, key_vectors, value_rows, cotangent):
    factor = 1.0 / math.sqrt(DH * SEQ)
    nblocks = SEQ // L_DEV
    blocks = tuple((arr.reshape(nblocks, L_DEV, HEADS * DH) for arr in (queries, key_vectors, value_rows, cotangent)))
    states, grads = lax.map(block_states, blocks)
    zeros_state = jnp.zeros((HEADS, DH, DH), jnp.float32)
    _, prefix = lax.scan(adding, zeros_state, states)
    _, suffix = lax.scan(adding, zeros_state, grads, reverse=True)

    def per_block(packed):
        return block_outputs(packed[0][0], packed[0][1], packed[0][2], packed[0][3], packed[1], packed[2], factor)
    outputs = lax.map(per_block, (blocks, prefix, suffix))
    return tuple((result.reshape(SEQ, HEADS * DH) for result in outputs))
```

```python
import functools
import math

import jax
import jax.numpy as jnp
from jax import lax
from jax.experimental import pallas as pl
from jax.experimental.pallas import tpu as pltpu
from jax.sharding import PartitionSpec as P

DH = 128
HEADS = 4
NX = 4
BLK = 256
HALF = DH // 2
MESH = pl.DeviceIdType.MESH


def inner_first(left, right):
    return lax.dot_general(
        left, right, (((0,), (0,)), ((), ())), preferred_element_type=jnp.float32
    )


def inner_last(left, right):
    return lax.dot_general(
        left, right, (((1,), (1,)), ((), ())), preferred_element_type=jnp.float32
    )


def plain(left, right):
    return jnp.dot(left, right, preferred_element_type=jnp.float32)


def split(state):
    upper = state.astype(jnp.bfloat16)
    lower = (state - upper.astype(jnp.float32)).astype(jnp.bfloat16)
    return upper, lower


def kernel(
    nz, factor,
    q_hbm, k_hbm, v_hbm, g_hbm,
    att_hbm, gq_hbm, gk_hbm, gv_hbm,
    q, k, v, g,
    acc, stage,
    state, row_in, row_out, total, col_in, col_out, column, entering,
    in_sem, out_sem,
    send1, recv1, send2, recv2, send3, recv3, send4, recv4,
):
    length = q.shape[0]
    blocks = length // BLK
    me = lax.axis_index("ctx")
    z = lax.div(me, NX)
    x = lax.rem(me, NX)
    sub = HALF // nz

    def along_x(i):
        return lax.rem(x + i, NX)

    def along_z(i):
        return lax.rem(z + i, nz)

    def at(zz, xx):
        return {"ctx": zz * NX + xx}

    loads = []
    for n, (src, dst) in enumerate(((k_hbm, k), (v_hbm, v), (q_hbm, q), (g_hbm, g))):
        copy = pltpu.make_async_copy(src, dst, in_sem.at[n])
        copy.start()
        loads.append(copy)

    barrier = pltpu.get_barrier_semaphore()
    for i in range(1, NX):
        pl.semaphore_signal(barrier, inc=1, device_id=at(z, along_x(i)), device_id_type=MESH)
    for i in range(1, nz):
        pl.semaphore_signal(barrier, inc=1, device_id=at(along_z(i), x), device_id_type=MESH)

    sends = []

    def rows(half):
        return pl.ds(half * HALF, HALF)

    def send(src, dst, ssem, rsem, device):
        copy = pltpu.make_async_remote_copy(
            src_ref=src, dst_ref=dst, send_sem=ssem, recv_sem=rsem,
            device_id=device, device_id_type=MESH,
        )
        copy.start()
        sends.append(copy)

    def arrived(ref, ssem, rsem):
        pltpu.make_async_remote_copy(
            src_ref=ref, dst_ref=ref, send_sem=ssem, recv_sem=rsem,
            device_id=at(z, along_x(1)), device_id_type=MESH,
        ).wait_recv()

    def cols(h):
        if isinstance(h, int):
            return pl.ds(h * DH, DH)
        return pl.ds(pl.multiple_of(h * DH, DH), DH)

    def states(st, left, right):
        for i in (1, 3, 2):
            h = along_x(i)
            state[st, i] = inner_first(left[:, cols(h)], right[:, cols(h)])
            if st == 0 and i == 1:
                pl.semaphore_wait(barrier, NX - 1 + nz - 1)
            for half in range(2):
                send(
                    state.at[st, i, rows(half)], row_in.at[st, x, rows(half)],
                    send1.at[st, half, i], recv1.at[st, half, x], at(z, h),
                )
        row_in[st, x] = inner_first(left[:, cols(x)], right[:, cols(x)])

    def row_scan(st, half):
        for i in (1, 3, 2):
            src = along_x(i)
            arrived(row_in.at[st, src, rows(half)], send1.at[st, half, i], recv1.at[st, half, src])
        order = list(range(NX)) if st == 0 else list(reversed(range(NX)))
        run = None
        for at_x in order:
            row_out[st, at_x, rows(half)] = (
                jnp.zeros((HALF, DH), jnp.float32) if run is None else run
            )
            new = row_in[st, at_x, rows(half)]
            run = new if run is None else run + new
        run = run.reshape(nz, sub, DH)
        total[st, half] = run
        for i in range(1, nz):
            dst = along_z(i)
            send(
                total.at[st, half, dst], col_in.at[st, half, z],
                send2.at[st, half, i], recv2.at[st, half, z], at(dst, x),
            )
        col_in[st, half, z] = total[st, half, z]

    def col_scan(st, half):
        for i in range(1, nz):
            src = along_z(i)
            arrived(col_in.at[st, half, src], send2.at[st, half, i], recv2.at[st, half, src])
        order = list(range(nz)) if st == 0 else list(reversed(range(nz)))
        run = jnp.zeros((sub, DH), jnp.float32)
        for at_z in order:
            col_out[st, half, at_z] = run
            run = run + col_in[st, half, at_z]
        for i in range(1, nz):
            dst = along_z(i)
            send(
                col_out.at[st, half, dst], column.at[st, half, z],
                send3.at[st, half, i], recv3.at[st, half, z], at(dst, x),
            )
        column[st, half, z] = col_out[st, half, z]

    def give_back(st, half):
        for i in range(1, nz):
            src = along_z(i)
            arrived(column.at[st, half, src], send3.at[st, half, i], recv3.at[st, half, src])
        base = column[st, half].reshape(HALF, DH)
        for at_x in range(NX):
            row_out[st, at_x, rows(half)] += base
        for i in (1, 3, 2):
            dst = along_x(i)
            send(
                row_out.at[st, dst, rows(half)], entering.at[st, x, rows(half)],
                send4.at[st, half, i], recv4.at[st, half, x], at(z, dst),
            )
        entering[st, x, rows(half)] = row_out[st, x, rows(half)]

    def take(st, half):
        for i in (1, 3, 2):
            src = along_x(i)
            arrived(
                entering.at[st, src, rows(half)], send4.at[st, half, i], recv4.at[st, half, src]
            )

    causal = lax.broadcasted_iota(jnp.int32, (BLK, BLK), 0) >= lax.broadcasted_iota(
        jnp.int32, (BLK, BLK), 1
    )

    def unit(h, r):
        c = cols(h)
        own = pl.ds(r * BLK, BLK)
        q_r, g_r = q[own, c], g[own, c]
        until = (r + 1) * BLK

        def lower(left, right):
            parts = []
            for b in range(r + 1):
                w = inner_last(left, right[pl.ds(b * BLK, BLK), c])
                if b == r:
                    w = jnp.where(causal, w, 0.0)
                parts.append(w.astype(jnp.bfloat16))
            return parts[0] if r == 0 else jnp.concatenate(parts, axis=1)

        weights = lower(q_r, k)
        back = lower(g_r, v)
        acc[0, own, c] = plain(weights, v[:until, c])
        acc[1, own, c] = plain(back, k[:until, c])
        for n, left, right in ((2, back, q_r), (3, weights, g_r)):
            add = inner_first(left, right)
            if r > 0:
                done = r * BLK
                acc[n, :done, c] += add[:done]
                acc[n, own, c] = add[done:]
            else:
                acc[n, own, c] = add

    outs = (att_hbm, gq_hbm, gk_hbm, gv_hbm)
    stores = []

    def finish(st, h):
        c = cols(h)
        hi, lo = split(entering[st, h])
        tall = jnp.concatenate([hi, lo], axis=0)
        wide = jnp.concatenate([hi, lo], axis=1)
        pairs = ((0, q, False), (1, g, True)) if st == 0 else ((3, k, False), (2, v, True))
        for n, left, across in pairs:
            for r in range(blocks):
                own = pl.ds(r * BLK, BLK)
                lhs = left[own, c]
                lhs = jnp.concatenate([lhs, lhs], axis=1)
                inter = inner_last(lhs, wide) if across else plain(lhs, tall)
                stage[n, own, c] = (factor * (acc[n, own, c] + inter)).astype(jnp.bfloat16)
            copy = pltpu.make_async_copy(
                stage.at[n, :, c], outs[n].at[:, c], out_sem.at[n, h]
            )
            copy.start()
            stores.append(copy)

    loads[0].wait()
    loads[1].wait()
    states(0, k, v)
    loads[2].wait()
    loads[3].wait()
    states(1, q, g)

    units = [(h, r) for h in range(HEADS) for r in range(blocks)]
    steps = [
        2, (row_scan, 0, 0), 1, (row_scan, 0, 1), 1, (row_scan, 1, 0), 1, (col_scan, 0, 0),
        (row_scan, 1, 1), 1, (col_scan, 0, 1), 1, (col_scan, 1, 0), 1, (give_back, 0, 0),
        (col_scan, 1, 1), 2, (give_back, 0, 1), 2, (give_back, 1, 0), 1, (give_back, 1, 1), 16,
        (take, 0, 0), (take, 0, 1),
    ]
    for step in steps:
        if isinstance(step, int):
            for _ in range(step):
                if units:
                    unit(*units.pop(0))
        else:
            step[0](*step[1:])
    for h in range(HEADS):
        finish(0, h)
    take(1, 0)
    take(1, 1)
    for h in range(HEADS):
        finish(1, h)
    for copy in sends:
        copy.wait_send()
    for copy in stores:
        copy.wait()


def solution(mesh):
    ctx = mesh.shape["ctx"]
    nz = ctx // NX
    sub = HALF // nz

    def on_device(queries, key_vectors, value_rows, cotangent):
        length, width = queries.shape
        factor = 1.0 / math.sqrt(DH * length * ctx)
        f32 = jnp.float32
        dma = pltpu.SemaphoreType.DMA
        out = jax.ShapeDtypeStruct((length, width), jnp.bfloat16)
        return pl.pallas_call(
            functools.partial(kernel, nz, factor),
            out_shape=(out,) * 4,
            in_specs=[pl.BlockSpec(memory_space=pltpu.HBM)] * 4,
            out_specs=(pl.BlockSpec(memory_space=OUT_SPACE),) * 4,
            scratch_shapes=[pltpu.VMEM((length, width), jnp.bfloat16)] * 4
            + [
                pltpu.VMEM((4, length, width), f32),
                pltpu.VMEM((4, length, width), jnp.bfloat16),
                pltpu.VMEM((2, NX, DH, DH), f32),
                pltpu.VMEM((2, NX, DH, DH), f32),
                pltpu.VMEM((2, NX, DH, DH), f32),
                pltpu.VMEM((2, 2, nz, sub, DH), f32),
                pltpu.VMEM((2, 2, nz, sub, DH), f32),
                pltpu.VMEM((2, 2, nz, sub, DH), f32),
                pltpu.VMEM((2, 2, nz, sub, DH), f32),
                pltpu.VMEM((2, NX, DH, DH), f32),
                dma((4,)),
                dma((4, HEADS)),
                dma((2, 2, NX)), dma((2, 2, NX)),
                dma((2, 2, nz)), dma((2, 2, nz)),
                dma((2, 2, nz)), dma((2, 2, nz)),
                dma((2, 2, NX)), dma((2, 2, NX)),
            ],
            compiler_params=pltpu.CompilerParams(
                collective_id=0, has_side_effects=True, vmem_limit_bytes=40 * 1024 * 1024
            ),
            name="linear_attention",
        )(queries, key_vectors, value_rows, cotangent)

    spec = P(("grp", "ctx"), None)
    return jax.shard_map(
        on_device, mesh=mesh, in_specs=(spec,) * 4, out_specs=(spec,) * 4, check_vma=False
    )


OUT_SPACE = pltpu.HBM
```

```python
import functools
import math

import jax
import jax.numpy as jnp
from jax import lax
from jax.experimental import pallas as pl
from jax.experimental.pallas import tpu as pltpu
from jax.sharding import PartitionSpec as P

DH = 128
HEADS = 4
NX = 4
BLK = 256
HALF = DH // 2
MESH = pl.DeviceIdType.MESH


def inner_first(left, right):
    return lax.dot_general(
        left, right, (((0,), (0,)), ((), ())), preferred_element_type=jnp.float32
    )


def inner_last(left, right):
    return lax.dot_general(
        left, right, (((1,), (1,)), ((), ())), preferred_element_type=jnp.float32
    )


def plain(left, right):
    return jnp.dot(left, right, preferred_element_type=jnp.float32)


def split(state):
    upper = state.astype(jnp.bfloat16)
    lower = (state - upper.astype(jnp.float32)).astype(jnp.bfloat16)
    return upper, lower


def kernel(
    nz, factor,
    q_hbm, k_hbm, v_hbm, g_hbm,
    att, gq, acc_k, acc_v, k, v, suffix,
    q, g, acc_a, acc_q,
    state, row_in, row_out, total, col_in, col_out, column, entering,
    in_sem,
    send1, recv1, send2, recv2, send3, recv3, send4, recv4,
):
    length = q.shape[0]
    blocks = length // BLK
    me = lax.axis_index("ctx")
    z = lax.div(me, NX)
    x = lax.rem(me, NX)
    grp = lax.axis_index("grp")
    core = lax.rem(grp, 2)
    scans = core == 1
    sub = HALF // nz

    def along_x(i):
        return lax.rem(x + i, NX)

    def along_z(i):
        return lax.rem(z + i, nz)

    def at(zz, xx, cc):
        return {"ctx": zz * NX + xx, "grp": grp - core + cc}

    def rows(half):
        return pl.ds(half * HALF, HALF)

    def cols(h):
        if isinstance(h, int):
            return pl.ds(h * DH, DH)
        return pl.ds(pl.multiple_of(h * DH, DH), DH)

    ORDER = (1, 3, 2, 0)
    loads = {}
    for n, (src, dst) in enumerate(((k_hbm, k), (v_hbm, v), (q_hbm, q), (g_hbm, g))):
        loads[n] = {}
    for pair in ((0, 1), (2, 3)):
        for i in ORDER:
            c = cols(along_x(i))
            for n in pair:
                src, dst = ((k_hbm, k), (v_hbm, v), (q_hbm, q), (g_hbm, g))[n]
                copy = pltpu.make_async_copy(src.at[:, c], dst.at[:, c], in_sem.at[n, i])
                copy.start()
                loads[n][i] = copy

    barrier = pltpu.get_barrier_semaphore()

    def greet(device):
        pl.semaphore_signal(barrier, inc=1, device_id=device, device_id_type=MESH)

    @pl.when(scans)
    def _():
        for i in range(1, NX):
            greet(at(z, along_x(i), 1))
        for i in range(NX):
            greet(at(z, along_x(i), 0))
        for i in range(1, nz):
            greet(at(along_z(i), x, 1))

    @pl.when(jnp.logical_not(scans))
    def _():
        for i in range(NX):
            greet(at(z, along_x(i), 1))

    def remote(src, dst, ssem, rsem, device):
        return pltpu.make_async_remote_copy(
            src_ref=src, dst_ref=dst, send_sem=ssem, recv_sem=rsem,
            device_id=device, device_id_type=MESH,
        )

    def arrived(ref, ssem, rsem):
        remote(ref, ref, ssem, rsem, at(z, along_x(1), 1)).wait_recv()

    def hand_in(st, half, i):
        return remote(
            state.at[st, i, rows(half)], row_in.at[core, st, x, rows(half)],
            send1.at[st, half, i], recv1.at[core, st, half, x], at(z, along_x(i), 1),
        )

    def states(st, left, right, arrays):
        for i in ORDER:
            h = along_x(i)
            for n in arrays:
                loads[n][i].wait()
            made = inner_first(left[:, cols(h)], right[:, cols(h)])
            state[st, i] = made
            if st == 0:
                if i == 1:
                    @pl.when(scans)
                    def _():
                        pl.semaphore_wait(barrier, 2 * NX - 1 + nz - 1)

                    @pl.when(jnp.logical_not(scans))
                    def _():
                        pl.semaphore_wait(barrier, NX)
                if i > 0:
                    for half in range(2):
                        hand_in(st, half, i).start()
                else:
                    hand_in_own(st, range(2))
        if st == 1:
            for half in range(2):
                for i in ORDER[:3]:
                    hand_in(st, half, i).start()
                hand_in_own(st, (half,))

    def hand_in_own(st, halves):
        @pl.when(scans)
        def _():
            for half in halves:
                row_in[1, st, x, rows(half)] = state[st, 0, rows(half)]

        @pl.when(jnp.logical_not(scans))
        def _():
            for half in halves:
                hand_in(st, half, 0).start()

    def hand_on(st, half, i):
        return remote(
            total.at[st, half, along_z(i)], col_in.at[st, half, z],
            send2.at[st, half, i], recv2.at[st, half, z], at(along_z(i), x, 1),
        )

    def row_scan(st, half):
        for cc in range(2):
            for i in ORDER[:3] if cc == 1 else ORDER:
                src = along_x(i)
                arrived(
                    row_in.at[cc, st, src, rows(half)],
                    send1.at[st, half, i], recv1.at[cc, st, half, src],
                )
        order = list(range(NX)) if st == 0 else list(reversed(range(NX)))
        for cc in range(2):
            run = None
            for at_x in order:
                row_out[cc, st, at_x, rows(half)] = (
                    jnp.zeros((HALF, DH), jnp.float32) if run is None else run
                )
                new = row_in[cc, st, at_x, rows(half)]
                run = new if run is None else run + new
            total[st, half, :, cc] = run.reshape(nz, sub, DH)
        for i in range(1, nz):
            hand_on(st, half, i).start()
        col_in[st, half, z] = total[st, half, z]

    def hand_down(st, half, i):
        return remote(
            col_out.at[st, half, along_z(i)], column.at[st, half, z],
            send3.at[st, half, i], recv3.at[st, half, z], at(along_z(i), x, 1),
        )

    def col_scan(st, half):
        for i in range(1, nz):
            src = along_z(i)
            arrived(col_in.at[st, half, src], send2.at[st, half, i], recv2.at[st, half, src])
        order = list(range(nz)) if st == 0 else list(reversed(range(nz)))
        run = jnp.zeros((2, sub, DH), jnp.float32)
        for at_z in order:
            col_out[st, half, at_z] = run
            run = run + col_in[st, half, at_z]
        for i in range(1, nz):
            hand_down(st, half, i).start()
        column[st, half, z] = col_out[st, half, z]

    def hand_back(st, half, cc, i):
        dst = along_x(i)
        return remote(
            row_out.at[cc, st, dst, rows(half)], entering.at[st, x, rows(half)],
            send4.at[cc, st, half, i], recv4.at[st, half, x], at(z, dst, cc),
        )

    def give_back(st, half):
        for i in range(1, nz):
            src = along_z(i)
            arrived(column.at[st, half, src], send3.at[st, half, i], recv3.at[st, half, src])
        for cc in range(2):
            base = column[st, half, :, cc].reshape(HALF, DH)
            for at_x in range(NX):
                row_out[cc, st, at_x, rows(half)] += base
            for i in ORDER if cc == 0 else ORDER[:3]:
                hand_back(st, half, cc, i).start()
        entering[st, x, rows(half)] = row_out[1, st, x, rows(half)]

    def take(st, half):
        for i in ORDER[:3]:
            src = along_x(i)
            arrived(
                entering.at[st, src, rows(half)], send4.at[0, st, half, i], recv4.at[st, half, src]
            )

        @pl.when(jnp.logical_not(scans))
        def _():
            arrived(entering.at[st, x, rows(half)], send4.at[0, st, half, 0], recv4.at[st, half, x])

    causal = lax.broadcasted_iota(jnp.int32, (BLK, BLK), 0) >= lax.broadcasted_iota(
        jnp.int32, (BLK, BLK), 1
    )

    def unit(h, r):
        c = cols(h)
        own = pl.ds(r * BLK, BLK)
        q_r, g_r = q[own, c], g[own, c]
        until = (r + 1) * BLK

        def lower(left, right):
            parts = []
            for b in range(r + 1):
                w = inner_last(left, right[pl.ds(b * BLK, BLK), c])
                if b == r:
                    w = jnp.where(causal, w, 0.0)
                parts.append(w.astype(jnp.bfloat16))
            return parts[0] if r == 0 else jnp.concatenate(parts, axis=1)

        weights = lower(q_r, k)
        back = lower(g_r, v)
        acc_a[own, c] = plain(weights, v[:until, c])
        acc_q[own, c] = plain(back, k[:until, c])
        for acc, left, right in ((acc_k, back, q_r), (acc_v, weights, g_r)):
            add = inner_first(left, right)
            if r > 0:
                done = r * BLK
                acc[:done, c] += add[:done]
                acc[own, c] = add[done:]
            else:
                acc[own, c] = add

    def finish(h):
        c = cols(h)
        hi, lo = split(entering[0, h])
        tall = jnp.concatenate([hi, lo], axis=0)
        wide = jnp.concatenate([hi, lo], axis=1)
        for out, acc, left in ((att, acc_a, q), (gq, acc_q, g)):
            for r in range(blocks):
                own = pl.ds(r * BLK, BLK)
                lhs = left[own, c]
                lhs = jnp.concatenate([lhs, lhs], axis=1)
                inter = plain(lhs, tall) if left is q else inner_last(lhs, wide)
                out[own, c] = (factor * (acc[own, c] + inter)).astype(jnp.bfloat16)

    states(0, k, v, (0, 1))
    states(1, q, g, (2, 3))

    units = [(h, r) for h in range(HEADS) for r in range(blocks)]
    steps = [
        3, (row_scan, 0, 0), (row_scan, 0, 1), 1, (row_scan, 1, 0), 1, (row_scan, 1, 1), 1,
        (col_scan, 0, 0), (col_scan, 0, 1), 1, (col_scan, 1, 0), 2, (col_scan, 1, 1), 1,
        (give_back, 0, 0), (give_back, 0, 1), 2, (give_back, 1, 0), 2, (give_back, 1, 1), 16,
    ]
    for step in steps:
        if isinstance(step, int):
            for _ in range(step):
                if units:
                    unit(*units.pop(0))
        else:
            pl.when(scans)(functools.partial(*step))
    take(0, 0)
    take(0, 1)
    for h in range(HEADS):
        finish(h)
    take(1, 0)
    take(1, 1)
    for h in range(HEADS):
        suffix[h, 0], suffix[h, 1] = split(entering[1, h])

    for st in range(2):
        for half in range(2):
            for i in range(1, NX):
                hand_in(st, half, i).wait_send()

    @pl.when(jnp.logical_not(scans))
    def _():
        for st in range(2):
            for half in range(2):
                hand_in(st, half, 0).wait_send()

    @pl.when(scans)
    def _():
        for st in range(2):
            for half in range(2):
                for i in range(1, nz):
                    hand_on(st, half, i).wait_send()
                    hand_down(st, half, i).wait_send()
                for i in range(NX):
                    hand_back(st, half, 0, i).wait_send()
                for i in range(1, NX):
                    hand_back(st, half, 1, i).wait_send()


def last_part(
    factor,
    att, gq, acc_k, acc_v, k, v, suffix,
    att_hbm, gq_hbm, gk_hbm, gv_hbm,
    gk, gv, sem,
):
    length = k.shape[0]
    copies = []

    def write(n, src, dst, part):
        copy = pltpu.make_async_copy(src.at[part], dst.at[part], sem.at[n, part.start // BLK])
        copy.start()
        copies.append(copy)

    parts = [pl.ds(r * BLK, BLK) for r in range(length // BLK)]
    for own in parts:
        write(0, att, att_hbm, own)
        write(1, gq, gq_hbm, own)
    for own in parts:
        for h in range(HEADS):
            c = pl.ds(h * DH, DH)
            tall = jnp.concatenate([suffix[h, 0], suffix[h, 1]], axis=0)
            wide = jnp.concatenate([suffix[h, 0], suffix[h, 1]], axis=1)
            lhs = k[own, c]
            inter = plain(jnp.concatenate([lhs, lhs], axis=1), tall)
            gv[own, c] = (factor * (acc_v[own, c] + inter)).astype(jnp.bfloat16)
            lhs = v[own, c]
            inter = inner_last(jnp.concatenate([lhs, lhs], axis=1), wide)
            gk[own, c] = (factor * (acc_k[own, c] + inter)).astype(jnp.bfloat16)
        write(2, gk, gk_hbm, own)
        write(3, gv, gv_hbm, own)
    for copy in copies:
        copy.wait()


def solution(mesh):
    ctx = mesh.shape["ctx"]
    nz = ctx // NX
    sub = HALF // nz

    def on_device(queries, key_vectors, value_rows, cotangent):
        length, width = queries.shape
        factor = 1.0 / math.sqrt(DH * length * ctx)
        f32, bf16 = jnp.float32, jnp.bfloat16
        dma = pltpu.SemaphoreType.DMA
        vmem, hbm = pltpu.VMEM, pltpu.HBM
        ready = pl.pallas_call(
            functools.partial(kernel, nz, factor),
            out_shape=(
                vmem((length, width), bf16),
                vmem((length, width), bf16),
                vmem((length, width), f32),
                vmem((length, width), f32),
                vmem((length, width), bf16),
                vmem((length, width), bf16),
                vmem((HEADS, 2, DH, DH), bf16),
            ),
            in_specs=[pl.BlockSpec(memory_space=hbm)] * 4,
            out_specs=(pl.BlockSpec(memory_space=vmem),) * 7,
            scratch_shapes=[
                vmem((length, width), bf16),
                vmem((length, width), bf16),
                vmem((length, width), f32),
                vmem((length, width), f32),
                vmem((2, NX, DH, DH), f32),
                vmem((2, 2, NX, DH, DH), f32),
                vmem((2, 2, NX, DH, DH), f32),
                vmem((2, 2, nz, 2, sub, DH), f32),
                vmem((2, 2, nz, 2, sub, DH), f32),
                vmem((2, 2, nz, 2, sub, DH), f32),
                vmem((2, 2, nz, 2, sub, DH), f32),
                vmem((2, NX, DH, DH), f32),
                dma((4, NX)),
                dma((2, 2, NX)), dma((2, 2, 2, NX)),
                dma((2, 2, nz)), dma((2, 2, nz)),
                dma((2, 2, nz)), dma((2, 2, nz)),
                dma((2, 2, 2, NX)), dma((2, 2, NX)),
            ],
            compiler_params=pltpu.CompilerParams(
                collective_id=0, has_side_effects=True, vmem_limit_bytes=32 * 1024 * 1024
            ),
            name="linear_attention",
        )(*(
            pltpu.with_memory_space_constraint(arr, hbm)
            for arr in (queries, key_vectors, value_rows, cotangent)
        ))
        out = jax.ShapeDtypeStruct((length, width), bf16)
        return pl.pallas_call(
            functools.partial(last_part, factor),
            out_shape=(out,) * 4,
            in_specs=[pl.BlockSpec(memory_space=vmem)] * 7,
            out_specs=(pl.BlockSpec(memory_space=hbm),) * 4,
            scratch_shapes=[
                vmem((length, width), bf16),
                vmem((length, width), bf16),
                dma((4, length // BLK)),
            ],
            compiler_params=pltpu.CompilerParams(vmem_limit_bytes=16 * 1024 * 1024),
            name="last_part",
        )(*(pltpu.with_memory_space_constraint(arr, vmem) for arr in ready))

    spec = P(("grp", "ctx"), None)
    return jax.shard_map(
        on_device, mesh=mesh, in_specs=(spec,) * 4, out_specs=(spec,) * 4, check_vma=False
    )
```

```python
import functools
import math

import jax
import jax.numpy as jnp
from jax import lax
from jax.experimental import pallas as pl
from jax.experimental.pallas import tpu as pltpu
from jax.sharding import PartitionSpec as P

DH = 128
HEADS = 4
NX = 4
BLK = 256
PIECES = 2
TALL = DH // PIECES
MESH = pl.DeviceIdType.MESH


def inner_first(left, right):
    return lax.dot_general(
        left, right, (((0,), (0,)), ((), ())), preferred_element_type=jnp.float32
    )


def inner_last(left, right):
    return lax.dot_general(
        left, right, (((1,), (1,)), ((), ())), preferred_element_type=jnp.float32
    )


def plain(left, right):
    return jnp.dot(left, right, preferred_element_type=jnp.float32)


def split(state):
    upper = state.astype(jnp.bfloat16)
    lower = (state - upper.astype(jnp.float32)).astype(jnp.bfloat16)
    return upper, lower


def kernel(
    nz, factor,
    q_hbm, k_hbm, v_hbm, g_hbm,
    att, gq, acc_k, acc_v, k, v, suffix,
    q, g, acc_a, acc_q,
    state, row_in, row_out, total, col_in, col_out, column, entering,
    in_sem, sent, got1, got2, got3, got4,
):
    length = q.shape[0]
    blocks = length // BLK
    me = lax.axis_index("ctx")
    z = lax.div(me, NX)
    x = lax.rem(me, NX)
    grp = lax.axis_index("grp")
    core = lax.rem(grp, 2)
    scans = core == 1
    sub = TALL // nz

    def along_x(i):
        return lax.rem(x + i, NX)

    def along_z(i):
        return lax.rem(z + i, nz)

    def at(zz, xx, cc):
        return {"ctx": zz * NX + xx, "grp": grp - core + cc}

    def rows(part):
        return pl.ds(part * TALL, TALL)

    def cols(h):
        if isinstance(h, int):
            return pl.ds(h * DH, DH)
        return pl.ds(pl.multiple_of(h * DH, DH), DH)

    loads = []
    for n, (src, dst) in enumerate(((k_hbm, k), (v_hbm, v), (q_hbm, q), (g_hbm, g))):
        copy = pltpu.make_async_copy(src, dst, in_sem.at[n])
        copy.start()
        loads.append(copy)

    barrier = pltpu.get_barrier_semaphore()

    def greet(device):
        pl.semaphore_signal(barrier, inc=1, device_id=device, device_id_type=MESH)

    @pl.when(scans)
    def _():
        for i in range(1, NX):
            greet(at(z, along_x(i), 1))
        for i in range(NX):
            greet(at(z, along_x(i), 0))
        for i in range(1, nz):
            greet(at(along_z(i), x, 1))

    @pl.when(jnp.logical_not(scans))
    def _():
        for i in range(NX):
            greet(at(z, along_x(i), 1))

    def send(src, dst, ssem, rsem, device):
        pltpu.make_async_remote_copy(
            src_ref=src, dst_ref=dst, send_sem=ssem, recv_sem=rsem,
            device_id=device, device_id_type=MESH,
        ).start()

    def arrived(ref, sem):
        pltpu.make_async_copy(ref, ref, sem).wait()

    ORDER = (1, 3, 2, 0)

    def hand_in(st, part, i):
        send(
            state.at[st, i, rows(part)], row_in.at[st, part, core * NX + x],
            sent.at[0], got1.at[st, part], at(z, along_x(i), 1),
        )

    def hand_in_own(st, part):
        @pl.when(scans)
        def _():
            row_in[st, part, NX + x] = state[st, 0, rows(part)]

        @pl.when(jnp.logical_not(scans))
        def _():
            hand_in(st, part, 0)

    def states(st, left, right):
        for i in ORDER:
            h = along_x(i)
            state[st, i] = inner_first(left[:, cols(h)], right[:, cols(h)])
            if st == 0:
                if i == 1:
                    @pl.when(scans)
                    def _():
                        pl.semaphore_wait(barrier, 2 * NX - 1 + nz - 1)

                    @pl.when(jnp.logical_not(scans))
                    def _():
                        pl.semaphore_wait(barrier, NX)
                for part in range(PIECES):
                    hand_in(st, part, i) if i > 0 else hand_in_own(st, part)
        if st == 1:
            for part in range(PIECES):
                for i in ORDER[:3]:
                    hand_in(st, part, i)
                hand_in_own(st, part)

    def row_scan(st, part):
        arrived(row_in.at[st, part, pl.ds(0, 2 * NX - 1)], got1.at[st, part])
        order = list(range(NX)) if st == 0 else list(reversed(range(NX)))
        for cc in range(2):
            run = None
            for at_x in order:
                row_out[cc, st, at_x, rows(part)] = (
                    jnp.zeros((TALL, DH), jnp.float32) if run is None else run
                )
                new = row_in[st, part, cc * NX + at_x]
                run = new if run is None else run + new
            total[st, part, :, cc] = run.reshape(nz, sub, DH)
        for i in range(1, nz):
            send(
                total.at[st, part, along_z(i)], col_in.at[st, part, z],
                sent.at[1], got2.at[st, part], at(along_z(i), x, 1),
            )
        col_in[st, part, z] = total[st, part, z]

    def col_scan(st, part):
        arrived(col_in.at[st, part, pl.ds(0, nz - 1)], got2.at[st, part])
        order = list(range(nz)) if st == 0 else list(reversed(range(nz)))
        run = jnp.zeros((2, sub, DH), jnp.float32)
        for at_z in order:
            col_out[st, part, at_z] = run
            run = run + col_in[st, part, at_z]
        for i in range(1, nz):
            send(
                col_out.at[st, part, along_z(i)], column.at[st, part, z],
                sent.at[2], got3.at[st, part], at(along_z(i), x, 1),
            )
        column[st, part, z] = col_out[st, part, z]

    def give_back(st, part):
        arrived(column.at[st, part, pl.ds(0, nz - 1)], got3.at[st, part])
        for cc in range(2):
            base = column[st, part, :, cc].reshape(TALL, DH)
            for at_x in range(NX):
                row_out[cc, st, at_x, rows(part)] += base
            for i in ORDER if cc == 0 else ORDER[:3]:
                send(
                    row_out.at[cc, st, along_x(i), rows(part)], entering.at[st, part, x],
                    sent.at[3 + cc], got4.at[st, part], at(z, along_x(i), cc),
                )
        entering[st, part, x] = row_out[1, st, x, rows(part)]

    def take(st, part):
        @pl.when(scans)
        def _():
            arrived(entering.at[st, part, pl.ds(0, NX - 1)], got4.at[st, part])

        @pl.when(jnp.logical_not(scans))
        def _():
            arrived(entering.at[st, part], got4.at[st, part])

    def entered(st, h):
        return jnp.concatenate([entering[st, part, h] for part in range(PIECES)], axis=0)

    causal = lax.broadcasted_iota(jnp.int32, (BLK, BLK), 0) >= lax.broadcasted_iota(
        jnp.int32, (BLK, BLK), 1
    )

    def unit(h, r):
        c = cols(h)
        own = pl.ds(r * BLK, BLK)
        q_r, g_r = q[own, c], g[own, c]
        until = (r + 1) * BLK

        def lower(left, right):
            parts = []
            for b in range(r + 1):
                w = inner_last(left, right[pl.ds(b * BLK, BLK), c])
                if b == r:
                    w = jnp.where(causal, w, 0.0)
                parts.append(w.astype(jnp.bfloat16))
            return parts[0] if r == 0 else jnp.concatenate(parts, axis=1)

        weights = lower(q_r, k)
        back = lower(g_r, v)
        acc_a[own, c] = plain(weights, v[:until, c])
        acc_q[own, c] = plain(back, k[:until, c])
        for acc, left, right in ((acc_k, back, q_r), (acc_v, weights, g_r)):
            add = inner_first(left, right)
            if r > 0:
                done = r * BLK
                acc[:done, c] += add[:done]
                acc[own, c] = add[done:]
            else:
                acc[own, c] = add

    def finish(h):
        c = cols(h)
        hi, lo = split(entered(0, h))
        tall = jnp.concatenate([hi, lo], axis=0)
        wide = jnp.concatenate([hi, lo], axis=1)
        for out, acc, left in ((att, acc_a, q), (gq, acc_q, g)):
            for r in range(blocks):
                own = pl.ds(r * BLK, BLK)
                lhs = left[own, c]
                lhs = jnp.concatenate([lhs, lhs], axis=1)
                inter = plain(lhs, tall) if left is q else inner_last(lhs, wide)
                out[own, c] = (factor * (acc[own, c] + inter)).astype(jnp.bfloat16)

    loads[0].wait()
    loads[1].wait()
    states(0, k, v)
    loads[2].wait()
    loads[3].wait()
    states(1, q, g)

    units = [(h, r) for h in range(HEADS) for r in range(blocks)]
    steps = [
        3, (row_scan, 0, 0), (row_scan, 0, 1), 1, (row_scan, 1, 0), 1, (row_scan, 1, 1), 1,
        (col_scan, 0, 0), (col_scan, 0, 1), 1, (col_scan, 1, 0), 2, (col_scan, 1, 1), 1,
        (give_back, 0, 0), (give_back, 0, 1), 2, (give_back, 1, 0), 2, (give_back, 1, 1), 16,
    ]
    for step in steps:
        if isinstance(step, int):
            for _ in range(step):
                if units:
                    unit(*units.pop(0))
        else:
            pl.when(scans)(functools.partial(*step))
    for part in range(PIECES):
        take(0, part)
    for h in range(HEADS):
        finish(h)
    for part in range(PIECES):
        take(1, part)
    for h in range(HEADS):
        suffix[h, 0], suffix[h, 1] = split(entered(1, h))

    def gone(ref, n):
        pltpu.make_async_copy(ref, ref, sent.at[n]).wait()

    @pl.when(scans)
    def _():
        gone(state.at[:, pl.ds(0, NX - 1)], 0)
        gone(total.at[:, :, pl.ds(0, nz - 1)], 1)
        gone(col_out.at[:, :, pl.ds(0, nz - 1)], 2)
        gone(row_out.at[0], 3)
        gone(row_out.at[1, :, pl.ds(0, NX - 1)], 4)

    @pl.when(jnp.logical_not(scans))
    def _():
        gone(state, 0)


def last_part(
    factor,
    att, gq, acc_k, acc_v, k, v, suffix,
    att_hbm, gq_hbm, gk_hbm, gv_hbm,
    gk, gv, sem,
):
    length = k.shape[0]
    copies = []

    def write(n, src, dst, part):
        copy = pltpu.make_async_copy(src.at[part], dst.at[part], sem.at[n, part.start // BLK])
        copy.start()
        copies.append(copy)

    parts = [pl.ds(r * BLK, BLK) for r in range(length // BLK)]
    for own in parts:
        write(0, att, att_hbm, own)
        write(1, gq, gq_hbm, own)
    for own in parts:
        for h in range(HEADS):
            c = pl.ds(h * DH, DH)
            tall = jnp.concatenate([suffix[h, 0], suffix[h, 1]], axis=0)
            wide = jnp.concatenate([suffix[h, 0], suffix[h, 1]], axis=1)
            lhs = k[own, c]
            inter = plain(jnp.concatenate([lhs, lhs], axis=1), tall)
            gv[own, c] = (factor * (acc_v[own, c] + inter)).astype(jnp.bfloat16)
            lhs = v[own, c]
            inter = inner_last(jnp.concatenate([lhs, lhs], axis=1), wide)
            gk[own, c] = (factor * (acc_k[own, c] + inter)).astype(jnp.bfloat16)
        write(2, gk, gk_hbm, own)
        write(3, gv, gv_hbm, own)
    for copy in copies:
        copy.wait()


def solution(mesh):
    ctx = mesh.shape["ctx"]
    nz = ctx // NX
    sub = TALL // nz

    def on_device(queries, key_vectors, value_rows, cotangent):
        length, width = queries.shape
        factor = 1.0 / math.sqrt(DH * length * ctx)
        f32, bf16 = jnp.float32, jnp.bfloat16
        dma = pltpu.SemaphoreType.DMA
        vmem, hbm = pltpu.VMEM, pltpu.HBM
        ready = pl.pallas_call(
            functools.partial(kernel, nz, factor),
            out_shape=(
                vmem((length, width), bf16),
                vmem((length, width), bf16),
                vmem((length, width), f32),
                vmem((length, width), f32),
                vmem((length, width), bf16),
                vmem((length, width), bf16),
                vmem((HEADS, 2, DH, DH), bf16),
            ),
            in_specs=[pl.BlockSpec(memory_space=hbm)] * 4,
            out_specs=(pl.BlockSpec(memory_space=vmem),) * 7,
            scratch_shapes=[
                vmem((length, width), bf16),
                vmem((length, width), bf16),
                vmem((length, width), f32),
                vmem((length, width), f32),
                vmem((2, NX, DH, DH), f32),
                vmem((2, PIECES, 2 * NX, TALL, DH), f32),
                vmem((2, 2, NX, DH, DH), f32),
                vmem((2, PIECES, nz, 2, sub, DH), f32),
                vmem((2, PIECES, nz, 2, sub, DH), f32),
                vmem((2, PIECES, nz, 2, sub, DH), f32),
                vmem((2, PIECES, nz, 2, sub, DH), f32),
                vmem((2, PIECES, NX, TALL, DH), f32),
                dma((4,)),
                dma((5,)),
                dma((2, PIECES)), dma((2, PIECES)), dma((2, PIECES)), dma((2, PIECES)),
            ],
            compiler_params=pltpu.CompilerParams(
                collective_id=0, has_side_effects=True, vmem_limit_bytes=32 * 1024 * 1024
            ),
            name="linear_attention",
        )(*(
            pltpu.with_memory_space_constraint(arr, hbm)
            for arr in (queries, key_vectors, value_rows, cotangent)
        ))
        out = jax.ShapeDtypeStruct((length, width), bf16)
        return pl.pallas_call(
            functools.partial(last_part, factor),
            out_shape=(out,) * 4,
            in_specs=[pl.BlockSpec(memory_space=vmem)] * 7,
            out_specs=(pl.BlockSpec(memory_space=hbm),) * 4,
            scratch_shapes=[
                vmem((length, width), bf16),
                vmem((length, width), bf16),
                dma((4, length // BLK)),
            ],
            compiler_params=pltpu.CompilerParams(vmem_limit_bytes=16 * 1024 * 1024),
            name="last_part",
        )(*(pltpu.with_memory_space_constraint(arr, vmem) for arr in ready))

    spec = P(("grp", "ctx"), None)
    return jax.shard_map(
        on_device, mesh=mesh, in_specs=(spec,) * 4, out_specs=(spec,) * 4, check_vma=False
    )
```

```python
import functools
import math

import jax
import jax.numpy as jnp
from jax import lax
from jax.experimental import pallas as pl
from jax.experimental.pallas import tpu as pltpu
from jax.sharding import PartitionSpec as P

DH = 128
HEADS = 4
NX = 4
BLK = 256
PIECES = 2
FEW = 3
TALL = DH // PIECES
MESH = pl.DeviceIdType.MESH


def inner_first(left, right):
    return lax.dot_general(
        left, right, (((0,), (0,)), ((), ())), preferred_element_type=jnp.float32
    )


def inner_last(left, right):
    return lax.dot_general(
        left, right, (((1,), (1,)), ((), ())), preferred_element_type=jnp.float32
    )


def plain(left, right):
    return jnp.dot(left, right, preferred_element_type=jnp.float32)


def split(state):
    upper = state.astype(jnp.bfloat16)
    lower = (state - upper.astype(jnp.float32)).astype(jnp.bfloat16)
    return upper, lower


def kernel(
    nz, factor,
    q_hbm, k_hbm, v_hbm, g_hbm,
    att, gq, acc_k, acc_v, k, v, suffix,
    q, g, acc_a, acc_q,
    state, row_in, row_out, total, col_in, col_out, column, entering,
    in_sem, sent, got1, got2, got3, got4, ready,
):
    length = q.shape[0]
    blocks = length // BLK
    me = lax.axis_index("ctx")
    z = lax.div(me, NX)
    x = lax.rem(me, NX)
    grp = lax.axis_index("grp")
    core = lax.rem(grp, 2)
    scans = core == 1
    sub = TALL // nz

    def along_x(i):
        return lax.rem(x + i, NX)

    def along_z(i):
        return lax.rem(z + i, nz)

    def at(zz, xx, cc):
        return {"ctx": zz * NX + xx, "grp": grp - core + cc}

    def rows(part):
        return pl.ds(part * TALL, TALL)

    def cols(h):
        if isinstance(h, int):
            return pl.ds(h * DH, DH)
        return pl.ds(pl.multiple_of(h * DH, DH), DH)

    early = z < FEW

    def load(n):
        src, dst = ((k_hbm, k), (v_hbm, v), (q_hbm, q), (g_hbm, g))[n]
        return pltpu.make_async_copy(src, dst, in_sem.at[n])

    @pl.when(early)
    def _():
        for n in (0, 1, 2, 3):
            load(n).start()

    @pl.when(jnp.logical_not(early))
    def _():
        for n in (2, 3, 0, 1):
            load(n).start()

    barrier = pltpu.get_barrier_semaphore()

    @pl.when(scans)
    def _():
        for i in range(NX):
            pl.semaphore_signal(barrier, inc=1, device_id=at(z, along_x(i), 0), device_id_type=MESH)
        for i in range(1, nz):
            pl.semaphore_signal(barrier, inc=1, device_id=at(along_z(i), x, 1), device_id_type=MESH)

    @pl.when(jnp.logical_not(scans))
    def _():
        pl.semaphore_wait(barrier, NX)
        pl.semaphore_signal(ready, inc=1, device_id=at(z, x, 1), device_id_type=MESH)

    def send(src, dst, ssem, rsem, device):
        pltpu.make_async_remote_copy(
            src_ref=src, dst_ref=dst, send_sem=ssem, recv_sem=rsem,
            device_id=device, device_id_type=MESH,
        ).start()

    def arrived(ref, sem):
        pltpu.make_async_copy(ref, ref, sem).wait()

    ORDER = (1, 3, 2, 0)

    def hand_in(st, part, i):
        send(
            state.at[st, i, rows(part)], row_in.at[st, part, core * NX + x],
            sent.at[0], got1.at[st, part], at(z, along_x(i), 1),
        )

    def hand_in_own(st, part):
        @pl.when(scans)
        def _():
            row_in[st, part, NX + x] = state[st, 0, rows(part)]

        @pl.when(jnp.logical_not(scans))
        def _():
            hand_in(st, part, 0)

    def states(st, first):
        left, right = ((k, v), (q, g))[st]
        load(2 * st).wait()
        load(2 * st + 1).wait()
        for i in ORDER:
            h = along_x(i)
            state[st, i] = inner_first(left[:, cols(h)], right[:, cols(h)])
            if first:
                if i == 1:
                    @pl.when(scans)
                    def _():
                        pl.semaphore_wait(ready, 1)
                for part in range(PIECES):
                    hand_in(st, part, i) if i > 0 else hand_in_own(st, part)
        if not first:
            for part in range(PIECES):
                for i in ORDER[:3]:
                    hand_in(st, part, i)
                hand_in_own(st, part)

    def row_scan(st, part, meet=False):
        arrived(row_in.at[st, part, pl.ds(0, 2 * NX - 1)], got1.at[st, part])
        order = list(range(NX)) if st == 0 else list(reversed(range(NX)))
        for cc in range(2):
            run = None
            for at_x in order:
                row_out[cc, st, at_x, rows(part)] = (
                    jnp.zeros((TALL, DH), jnp.float32) if run is None else run
                )
                new = row_in[st, part, cc * NX + at_x]
                run = new if run is None else run + new
            total[st, part, :, cc] = run.reshape(nz, sub, DH)
        if meet:
            pl.semaphore_wait(barrier, nz - 1)
        for i in range(1, nz):
            send(
                total.at[st, part, along_z(i)], col_in.at[st, part, z],
                sent.at[1], got2.at[st, part, jnp.where(early, 0, 1)], at(along_z(i), x, 1),
            )
        col_in[st, part, z] = total[st, part, z]

    def heard(st, part, few):
        group = got2.at[st, part, 0 if few else 1]
        among = FEW if few else nz - FEW
        inside = early if few else jnp.logical_not(early)

        @pl.when(inside)
        def _():
            arrived(col_in.at[st, part, pl.ds(0, among - 1)], group)

        @pl.when(jnp.logical_not(inside))
        def _():
            arrived(col_in.at[st, part, pl.ds(0, among)], group)

    def tell(st, part, dst):
        @pl.when(z != dst)
        def _():
            send(
                col_out.at[st, part, dst], column.at[st, part, z],
                sent.at[2], got3.at[st, part], at(dst, x, 1),
            )

    def col_scan(part):
        heard(1, part, True)
        heard(1, part, False)
        run = jnp.zeros((2, sub, DH), jnp.float32)
        for at_z in reversed(range(nz)):
            col_out[1, part, at_z] = run
            run = run + col_in[1, part, at_z]
        for at_z in range(nz):
            tell(1, part, at_z)
        column[1, part, z] = col_out[1, part, z]

    def col_scan_few(part):
        heard(0, part, True)
        run = jnp.zeros((2, sub, DH), jnp.float32)
        for at_z in range(FEW):
            run = run + col_in[0, part, at_z]
            col_out[0, part, at_z + 1] = run
        for at_z in range(1, FEW + 1):
            tell(0, part, at_z)

    def col_scan_rest(part):
        heard(0, part, False)
        run = col_out[0, part, FEW]
        for at_z in range(FEW, nz - 1):
            run = run + col_in[0, part, at_z]
            col_out[0, part, at_z + 1] = run
        for at_z in range(FEW + 1, nz):
            tell(0, part, at_z)

    def give_back(st, part, alone=False):
        if not alone:
            if st == 0:
                column[0, part, z] = col_out[0, part, z]
            arrived(column.at[st, part, pl.ds(0, nz - 1)], got3.at[st, part])
        for cc in range(2):
            if not alone:
                base = column[st, part, :, cc].reshape(TALL, DH)
            for i in (2, 1, 3, 0):
                here = row_out.at[cc, st, along_x(i), rows(part)]
                if not alone:
                    here[...] += base
                if cc == 0 or i > 0:
                    send(
                        here, entering.at[st, part, x],
                        sent.at[3 + cc], got4.at[st, part], at(z, along_x(i), cc),
                    )
        entering[st, part, x] = row_out[1, st, x, rows(part)]

    def give_first(part):
        @pl.when(z == 0)
        def _():
            give_back(0, part, True)

    def give_few(part):
        @pl.when(jnp.logical_and(z > 0, z <= FEW))
        def _():
            give_back(0, part)

    def give_rest(part):
        @pl.when(z > FEW)
        def _():
            give_back(0, part)

    def take(st, part):
        @pl.when(scans)
        def _():
            arrived(entering.at[st, part, pl.ds(0, NX - 1)], got4.at[st, part])

        @pl.when(jnp.logical_not(scans))
        def _():
            arrived(entering.at[st, part], got4.at[st, part])

    def entered(st, h):
        return jnp.concatenate([entering[st, part, h] for part in range(PIECES)], axis=0)

    causal = lax.broadcasted_iota(jnp.int32, (BLK, BLK), 0) >= lax.broadcasted_iota(
        jnp.int32, (BLK, BLK), 1
    )

    def unit(h, r):
        c = cols(h)
        own = pl.ds(r * BLK, BLK)
        q_r, g_r = q[own, c], g[own, c]
        until = (r + 1) * BLK

        def lower(left, right):
            parts = []
            for b in range(r + 1):
                w = inner_last(left, right[pl.ds(b * BLK, BLK), c])
                if b == r:
                    w = jnp.where(causal, w, 0.0)
                parts.append(w.astype(jnp.bfloat16))
            return parts[0] if r == 0 else jnp.concatenate(parts, axis=1)

        weights = lower(q_r, k)
        back = lower(g_r, v)
        acc_a[own, c] = plain(weights, v[:until, c])
        acc_q[own, c] = plain(back, k[:until, c])
        for acc, left, right in ((acc_k, back, q_r), (acc_v, weights, g_r)):
            add = inner_first(left, right)
            if r > 0:
                done = r * BLK
                acc[:done, c] += add[:done]
                acc[own, c] = add[done:]
            else:
                acc[own, c] = add

    def finish(h):
        c = cols(h)
        hi, lo = split(entered(0, h))
        tall = jnp.concatenate([hi, lo], axis=0)
        wide = jnp.concatenate([hi, lo], axis=1)
        for out, acc, left in ((att, acc_a, q), (gq, acc_q, g)):
            for r in range(blocks):
                own = pl.ds(r * BLK, BLK)
                lhs = left[own, c]
                lhs = jnp.concatenate([lhs, lhs], axis=1)
                inter = plain(lhs, tall) if left is q else inner_last(lhs, wide)
                out[own, c] = (factor * (acc[own, c] + inter)).astype(jnp.bfloat16)

    @pl.when(early)
    def _():
        states(0, True)
        states(1, False)

    @pl.when(jnp.logical_not(early))
    def _():
        states(1, True)
        states(0, False)

    def first_scans():
        @pl.when(early)
        def _():
            for part in range(PIECES):
                row_scan(0, part, part == 0)

        @pl.when(jnp.logical_not(early))
        def _():
            for part in range(PIECES):
                row_scan(1, part, part == 0)

    def second_scans():
        @pl.when(early)
        def _():
            for part in range(PIECES):
                row_scan(1, part)
            for part in range(PIECES):
                give_first(part)
            for part in range(PIECES):
                col_scan_few(part)

        @pl.when(jnp.logical_not(early))
        def _():
            for part in range(PIECES):
                col_scan_few(part)
            for part in range(PIECES):
                row_scan(0, part)

    units = [(h, r) for h in range(HEADS) for r in range(blocks)]
    steps = [
        6, (first_scans,), 3, (second_scans,), (col_scan, 0), (col_scan, 1), 3,
        (give_few, 0), (give_few, 1), (col_scan_rest, 0), (col_scan_rest, 1), 1,
        (give_back, 1, 0), (give_back, 1, 1), 2, (give_rest, 0), (give_rest, 1), 16,
    ]
    for step in steps:
        if isinstance(step, int):
            for _ in range(step):
                if units:
                    unit(*units.pop(0))
        else:
            pl.when(scans)(functools.partial(*step))
    for part in range(PIECES):
        take(0, part)
    for h in range(HEADS):
        finish(h)
    for part in range(PIECES):
        take(1, part)
    for h in range(HEADS):
        suffix[h, 0], suffix[h, 1] = split(entered(1, h))

    def gone(ref, n):
        pltpu.make_async_copy(ref, ref, sent.at[n]).wait()

    @pl.when(scans)
    def _():
        gone(state.at[:, pl.ds(0, NX - 1)], 0)
        gone(total.at[:, :, pl.ds(0, nz - 1)], 1)
        gone(col_out.at[1, :, pl.ds(0, nz - 1)], 2)
        gone(col_out.at[0, :, pl.ds(0, nz - 2)], 2)

        @pl.when(z == 0)
        def _():
            gone(col_out.at[0, :, nz - 1], 2)

        gone(row_out.at[0], 3)
        gone(row_out.at[1, :, pl.ds(0, NX - 1)], 4)

    @pl.when(jnp.logical_not(scans))
    def _():
        gone(state, 0)


def last_part(
    factor,
    att, gq, acc_k, acc_v, k, v, suffix,
    att_hbm, gq_hbm, gk_hbm, gv_hbm,
    gk, gv, sem,
):
    length = k.shape[0]
    copies = []

    def write(n, src, dst, part):
        copy = pltpu.make_async_copy(src.at[part], dst.at[part], sem.at[n, part.start // BLK])
        copy.start()
        copies.append(copy)

    parts = [pl.ds(r * BLK, BLK) for r in range(length // BLK)]
    for own in parts:
        write(0, att, att_hbm, own)
        write(1, gq, gq_hbm, own)
    for own in parts:
        for h in range(HEADS):
            c = pl.ds(h * DH, DH)
            tall = jnp.concatenate([suffix[h, 0], suffix[h, 1]], axis=0)
            wide = jnp.concatenate([suffix[h, 0], suffix[h, 1]], axis=1)
            lhs = k[own, c]
            inter = plain(jnp.concatenate([lhs, lhs], axis=1), tall)
            gv[own, c] = (factor * (acc_v[own, c] + inter)).astype(jnp.bfloat16)
            lhs = v[own, c]
            inter = inner_last(jnp.concatenate([lhs, lhs], axis=1), wide)
            gk[own, c] = (factor * (acc_k[own, c] + inter)).astype(jnp.bfloat16)
        write(2, gk, gk_hbm, own)
        write(3, gv, gv_hbm, own)
    for copy in copies:
        copy.wait()


def solution(mesh):
    ctx = mesh.shape["ctx"]
    nz = ctx // NX
    sub = TALL // nz

    def on_device(queries, key_vectors, value_rows, cotangent):
        length, width = queries.shape
        factor = 1.0 / math.sqrt(DH * length * ctx)
        f32, bf16 = jnp.float32, jnp.bfloat16
        dma = pltpu.SemaphoreType.DMA
        vmem, hbm = pltpu.VMEM, pltpu.HBM
        ready = pl.pallas_call(
            functools.partial(kernel, nz, factor),
            out_shape=(
                vmem((length, width), bf16),
                vmem((length, width), bf16),
                vmem((length, width), f32),
                vmem((length, width), f32),
                vmem((length, width), bf16),
                vmem((length, width), bf16),
                vmem((HEADS, 2, DH, DH), bf16),
            ),
            in_specs=[pl.BlockSpec(memory_space=hbm)] * 4,
            out_specs=(pl.BlockSpec(memory_space=vmem),) * 7,
            scratch_shapes=[
                vmem((length, width), bf16),
                vmem((length, width), bf16),
                vmem((length, width), f32),
                vmem((length, width), f32),
                vmem((2, NX, DH, DH), f32),
                vmem((2, PIECES, 2 * NX, TALL, DH), f32),
                vmem((2, 2, NX, DH, DH), f32),
                vmem((2, PIECES, nz, 2, sub, DH), f32),
                vmem((2, PIECES, nz, 2, sub, DH), f32),
                vmem((2, PIECES, nz, 2, sub, DH), f32),
                vmem((2, PIECES, nz, 2, sub, DH), f32),
                vmem((2, PIECES, NX, TALL, DH), f32),
                dma((4,)),
                dma((5,)),
                dma((2, PIECES)), dma((2, PIECES, 2)), dma((2, PIECES)), dma((2, PIECES)),
                pltpu.SemaphoreType.REGULAR,
            ],
            compiler_params=pltpu.CompilerParams(
                collective_id=0, has_side_effects=True, vmem_limit_bytes=32 * 1024 * 1024
            ),
            name="linear_attention",
        )(*(
            pltpu.with_memory_space_constraint(arr, hbm)
            for arr in (queries, key_vectors, value_rows, cotangent)
        ))
        out = jax.ShapeDtypeStruct((length, width), bf16)
        return pl.pallas_call(
            functools.partial(last_part, factor),
            out_shape=(out,) * 4,
            in_specs=[pl.BlockSpec(memory_space=vmem)] * 7,
            out_specs=(pl.BlockSpec(memory_space=hbm),) * 4,
            scratch_shapes=[
                vmem((length, width), bf16),
                vmem((length, width), bf16),
                dma((4, length // BLK)),
            ],
            compiler_params=pltpu.CompilerParams(vmem_limit_bytes=16 * 1024 * 1024),
            name="last_part",
        )(*(pltpu.with_memory_space_constraint(arr, vmem) for arr in ready))

    spec = P(("grp", "ctx"), None)
    return jax.shard_map(
        on_device, mesh=mesh, in_specs=(spec,) * 4, out_specs=(spec,) * 4, check_vma=False
    )
```

```python
import functools
import math

import jax
import jax.numpy as jnp
from jax import lax
from jax.experimental import pallas as pl
from jax.experimental.pallas import tpu as pltpu
from jax.sharding import PartitionSpec as P

DH = 128
HEADS = 4
NX = 4
BLK = 256
PIECES = 2
FEW = 3
TALL = DH // PIECES
MESH = pl.DeviceIdType.MESH


def inner_first(left, right):
    return lax.dot_general(
        left, right, (((0,), (0,)), ((), ())), preferred_element_type=jnp.float32
    )


def inner_last(left, right):
    return lax.dot_general(
        left, right, (((1,), (1,)), ((), ())), preferred_element_type=jnp.float32
    )


def plain(left, right):
    return jnp.dot(left, right, preferred_element_type=jnp.float32)


def split(state):
    upper = state.astype(jnp.bfloat16)
    lower = (state - upper.astype(jnp.float32)).astype(jnp.bfloat16)
    return upper, lower


def inter_last(factor, out, acc, left, hi, lo, across, c, parts):
    both = jnp.concatenate([hi, lo], axis=1 if across else 0)
    for r in parts:
        own = pl.ds(r * BLK, BLK)
        lhs = left[own, c]
        lhs = jnp.concatenate([lhs, lhs], axis=1)
        inter = inner_last(lhs, both) if across else plain(lhs, both)
        out[own, c] = (factor * (acc[own, c] + inter)).astype(jnp.bfloat16)


def kernel(
    nz, factor,
    q_hbm, k_hbm, v_hbm, g_hbm,
    done_a, done_b, acc_a, acc_q, acc_k, acc_v, q, k, v, g, open_state,
    state, row_in, row_out, total, col_in, col_out, column, entering,
    in_sem, sent, got1, got2, got3, got4, ready,
):
    length = q.shape[0]
    blocks = length // BLK
    me = lax.axis_index("ctx")
    z = lax.div(me, NX)
    x = lax.rem(me, NX)
    grp = lax.axis_index("grp")
    core = lax.rem(grp, 2)
    scans = core == 1
    sub = TALL // nz

    def along_x(i):
        return lax.rem(x + i, NX)

    def along_z(i):
        return lax.rem(z + i, nz)

    def at(zz, xx, cc):
        return {"ctx": zz * NX + xx, "grp": grp - core + cc}

    def rows(part):
        return pl.ds(part * TALL, TALL)

    def cols(h):
        if isinstance(h, int):
            return pl.ds(h * DH, DH)
        return pl.ds(pl.multiple_of(h * DH, DH), DH)

    early = z < FEW

    ORDER = (1, 3, 2, 0)
    pairs = ((k_hbm, k), (v_hbm, v), (q_hbm, q), (g_hbm, g))

    def load_all(n):
        src, dst = pairs[n]
        return pltpu.make_async_copy(src, dst, in_sem.at[n % 2, NX])

    def load_head(n, i):
        src, dst = pairs[n]
        c = cols(along_x(i))
        return pltpu.make_async_copy(src.at[:, c], dst.at[:, c], in_sem.at[n % 2, i])

    def load(first, second):
        for i in ORDER:
            for n in first:
                load_head(n, i).start()
        for n in second:
            load_all(n).start()

    @pl.when(early)
    def _():
        load((0, 1), (2, 3))

    @pl.when(jnp.logical_not(early))
    def _():
        load((2, 3), (0, 1))

    barrier = pltpu.get_barrier_semaphore()

    @pl.when(scans)
    def _():
        for i in range(NX):
            pl.semaphore_signal(barrier, inc=1, device_id=at(z, along_x(i), 0), device_id_type=MESH)
        for i in range(1, nz):
            pl.semaphore_signal(barrier, inc=1, device_id=at(along_z(i), x, 1), device_id_type=MESH)

    @pl.when(jnp.logical_not(scans))
    def _():
        pl.semaphore_wait(barrier, NX)
        pl.semaphore_signal(ready, inc=1, device_id=at(z, x, 1), device_id_type=MESH)

    def send(src, dst, ssem, rsem, device):
        pltpu.make_async_remote_copy(
            src_ref=src, dst_ref=dst, send_sem=ssem, recv_sem=rsem,
            device_id=device, device_id_type=MESH,
        ).start()

    def arrived(ref, sem):
        pltpu.make_async_copy(ref, ref, sem).wait()

    def hand_in(st, part, i):
        send(
            state.at[st, i, rows(part)], row_in.at[st, part, core * NX + x],
            sent.at[0], got1.at[st, part], at(z, along_x(i), 1),
        )

    def hand_in_own(st, part):
        @pl.when(scans)
        def _():
            row_in[st, part, NX + x] = state[st, 0, rows(part)]

        @pl.when(jnp.logical_not(scans))
        def _():
            hand_in(st, part, 0)

    def states(st, first):
        left, right = ((k, v), (q, g))[st]
        if not first:
            load_all(2 * st).wait()
            load_all(2 * st + 1).wait()
        for i in ORDER:
            h = along_x(i)
            if first:
                load_head(2 * st, i).wait()
                load_head(2 * st + 1, i).wait()
            state[st, i] = inner_first(left[:, cols(h)], right[:, cols(h)])
            if first:
                if i == 1:
                    @pl.when(scans)
                    def _():
                        pl.semaphore_wait(ready, 1)
                hand_in(st, 0, i) if i > 0 else hand_in_own(st, 0)
        for part in range(1 if first else 0, PIECES):
            for i in ORDER[:3]:
                hand_in(st, part, i)
            hand_in_own(st, part)

    def row_scan(st, part, meet=False):
        arrived(row_in.at[st, part, pl.ds(0, 2 * NX - 1)], got1.at[st, part])
        order = list(range(NX)) if st == 0 else list(reversed(range(NX)))
        for cc in range(2):
            run = None
            for at_x in order:
                row_out[cc, st, at_x, rows(part)] = (
                    jnp.zeros((TALL, DH), jnp.float32) if run is None else run
                )
                new = row_in[st, part, cc * NX + at_x]
                run = new if run is None else run + new
            total[st, part, :, cc] = run.reshape(nz, sub, DH)
        if meet:
            pl.semaphore_wait(barrier, nz - 1)
        for i in range(1, nz):
            send(
                total.at[st, part, along_z(i)], col_in.at[st, part, z],
                sent.at[1], got2.at[st, part, jnp.where(early, 0, 1)], at(along_z(i), x, 1),
            )
        col_in[st, part, z] = total[st, part, z]

    def heard(st, part, few):
        group = got2.at[st, part, 0 if few else 1]
        among = FEW if few else nz - FEW
        inside = early if few else jnp.logical_not(early)

        @pl.when(inside)
        def _():
            arrived(col_in.at[st, part, pl.ds(0, among - 1)], group)

        @pl.when(jnp.logical_not(inside))
        def _():
            arrived(col_in.at[st, part, pl.ds(0, among)], group)

    def tell(st, part, dst):
        @pl.when(z != dst)
        def _():
            send(
                col_out.at[st, part, dst], column.at[st, part, z],
                sent.at[2], got3.at[st, part], at(dst, x, 1),
            )

    def col_scan(part):
        heard(1, part, True)
        heard(1, part, False)
        run = jnp.zeros((2, sub, DH), jnp.float32)
        for at_z in reversed(range(nz)):
            col_out[1, part, at_z] = run
            run = run + col_in[1, part, at_z]
        for at_z in range(nz):
            tell(1, part, at_z)
        column[1, part, z] = col_out[1, part, z]

    def col_scan_few(part):
        heard(0, part, True)
        run = jnp.zeros((2, sub, DH), jnp.float32)
        for at_z in range(FEW):
            run = run + col_in[0, part, at_z]
            col_out[0, part, at_z + 1] = run
        for at_z in range(1, FEW + 1):
            tell(0, part, at_z)

    def col_scan_rest(part):
        heard(0, part, False)
        run = col_out[0, part, FEW]
        for at_z in range(FEW, nz - 1):
            run = run + col_in[0, part, at_z]
            col_out[0, part, at_z + 1] = run
        for at_z in range(FEW + 1, nz):
            tell(0, part, at_z)

    def give_back(st, part, alone=False):
        if not alone:
            if st == 0:
                column[0, part, z] = col_out[0, part, z]
            arrived(column.at[st, part, pl.ds(0, nz - 1)], got3.at[st, part])
        for cc in range(2):
            if not alone:
                base = column[st, part, :, cc].reshape(TALL, DH)
            for i in (2, 1, 3, 0):
                here = row_out.at[cc, st, along_x(i), rows(part)]
                if not alone:
                    here[...] += base
                if cc == 0 or i > 0:
                    send(
                        here, entering.at[st, part, x],
                        sent.at[3 + cc], got4.at[st, part], at(z, along_x(i), cc),
                    )
        entering[st, part, x] = row_out[1, st, x, rows(part)]

    def give_first(part):
        @pl.when(z == 0)
        def _():
            give_back(0, part, True)

    def give_few(part):
        @pl.when(jnp.logical_and(z > 0, z <= FEW))
        def _():
            give_back(0, part)

    def give_rest(part):
        @pl.when(z > FEW)
        def _():
            give_back(0, part)

    def take(st, part):
        @pl.when(scans)
        def _():
            arrived(entering.at[st, part, pl.ds(0, NX - 1)], got4.at[st, part])

        @pl.when(jnp.logical_not(scans))
        def _():
            arrived(entering.at[st, part], got4.at[st, part])

    def entered(st, h):
        return jnp.concatenate([entering[st, part, h] for part in range(PIECES)], axis=0)

    causal = lax.broadcasted_iota(jnp.int32, (BLK, BLK), 0) >= lax.broadcasted_iota(
        jnp.int32, (BLK, BLK), 1
    )

    def unit(h, r):
        c = cols(h)
        own = pl.ds(r * BLK, BLK)
        q_r, g_r = q[own, c], g[own, c]
        until = (r + 1) * BLK

        def lower(left, right):
            parts = []
            for b in range(r + 1):
                w = inner_last(left, right[pl.ds(b * BLK, BLK), c])
                if b == r:
                    w = jnp.where(causal, w, 0.0)
                parts.append(w.astype(jnp.bfloat16))
            return parts[0] if r == 0 else jnp.concatenate(parts, axis=1)

        weights = lower(q_r, k)
        back = lower(g_r, v)
        acc_a[own, c] = plain(weights, v[:until, c])
        acc_q[own, c] = plain(back, k[:until, c])
        for acc, left, right in ((acc_k, back, q_r), (acc_v, weights, g_r)):
            add = inner_first(left, right)
            if r > 0:
                done = r * BLK
                acc[:done, c] += add[:done]
                acc[own, c] = add[done:]
            else:
                acc[own, c] = add

    def finish(st, h):
        c = cols(h)
        hi, lo = split(entered(st, h))
        accs = ((acc_a, acc_q), (acc_v, acc_k))[st]
        lefts = ((q, g), (k, v))[st]
        for out, acc, left, across in zip((done_a, done_b), accs, lefts, (False, True)):
            inter_last(factor, out, acc, left, hi, lo, across, c, range(blocks))

    def leave(st):
        for h in range(HEADS):
            open_state[h, 0], open_state[h, 1] = split(entered(st, h))

    @pl.when(early)
    def _():
        states(0, True)
        states(1, False)

    @pl.when(jnp.logical_not(early))
    def _():
        states(1, True)
        states(0, False)

    def first_scans():
        @pl.when(early)
        def _():
            for part in range(PIECES):
                row_scan(0, part, part == 0)

        @pl.when(jnp.logical_not(early))
        def _():
            for part in range(PIECES):
                row_scan(1, part, part == 0)

    def second_scans():
        @pl.when(early)
        def _():
            for part in range(PIECES):
                row_scan(1, part)
            for part in range(PIECES):
                give_first(part)
            for part in range(PIECES):
                col_scan_few(part)

        @pl.when(jnp.logical_not(early))
        def _():
            for part in range(PIECES):
                col_scan_few(part)
            for part in range(PIECES):
                row_scan(0, part)

    def third_scans():
        @pl.when(early)
        def _():
            for part in range(PIECES):
                give_back(1, part)
                col_scan_rest(part)

        @pl.when(jnp.logical_not(early))
        def _():
            for part in range(PIECES):
                col_scan_rest(part)
            for part in range(PIECES):
                give_back(1, part)

    units = [(h, r) for h in range(HEADS) for r in range(blocks)]
    steps = [
        6, (first_scans,), 1, (second_scans,), (col_scan, 0), (col_scan, 1), (give_few, 0), (give_few, 1), 4,
        (third_scans,), (give_rest, 0), (give_rest, 1), 16,
    ]
    for step in steps:
        if isinstance(step, int):
            for _ in range(step):
                if units:
                    unit(*units.pop(0))
        else:
            pl.when(scans)(functools.partial(*step))
    for near, order in ((z <= FEW, (0, 1)), (z > FEW, (1, 0))):
        @pl.when(near)
        def _():
            for part in range(PIECES):
                take(order[0], part)
            for h in range(HEADS):
                finish(order[0], h)
            for part in range(PIECES):
                take(order[1], part)
            leave(order[1])

    def gone(ref, n):
        pltpu.make_async_copy(ref, ref, sent.at[n]).wait()

    @pl.when(scans)
    def _():
        gone(state.at[:, pl.ds(0, NX - 1)], 0)
        gone(total.at[:, :, pl.ds(0, nz - 1)], 1)
        gone(col_out.at[1, :, pl.ds(0, nz - 1)], 2)
        gone(col_out.at[0, :, pl.ds(0, nz - 2)], 2)

        @pl.when(z == 0)
        def _():
            gone(col_out.at[0, :, nz - 1], 2)

        gone(row_out.at[0], 3)
        gone(row_out.at[1, :, pl.ds(0, NX - 1)], 4)

    @pl.when(jnp.logical_not(scans))
    def _():
        gone(state, 0)


def last_part(
    factor,
    done_a, done_b, acc_a, acc_q, acc_k, acc_v, q, k, v, g, open_state,
    att_hbm, gq_hbm, gk_hbm, gv_hbm,
    late_a, late_b, sem,
):
    blocks = k.shape[0] // BLK
    z = lax.div(lax.axis_index("ctx"), NX)

    def write(n, src, dst, r):
        part = pl.ds(r * BLK, BLK)
        return pltpu.make_async_copy(src.at[part], dst.at[part], sem.at[n])

    def rest(first, second, accs, lefts):
        copies = []
        for r in range(blocks):
            copies.append(write(0, done_a, first[0], r))
            copies.append(write(1, done_b, first[1], r))
        for copy in copies:
            copy.start()
        for r in range(blocks):
            for h in range(HEADS):
                c = pl.ds(h * DH, DH)
                hi, lo = open_state[h, 0], open_state[h, 1]
                for out, acc, left, across in zip((late_a, late_b), accs, lefts, (False, True)):
                    inter_last(factor, out, acc, left, hi, lo, across, c, (r,))
            for n, src in ((2, late_a), (3, late_b)):
                copy = write(n, src, second[n - 2], r)
                copy.start()
                copies.append(copy)
        for n, src in enumerate((done_a, done_b, late_a, late_b)):
            pltpu.make_async_copy(src, src, sem.at[n]).wait()

    @pl.when(z <= FEW)
    def _():
        rest((att_hbm, gq_hbm), (gv_hbm, gk_hbm), (acc_v, acc_k), (k, v))

    @pl.when(z > FEW)
    def _():
        rest((gv_hbm, gk_hbm), (att_hbm, gq_hbm), (acc_a, acc_q), (q, g))


def solution(mesh):
    ctx = mesh.shape["ctx"]
    nz = ctx // NX
    sub = TALL // nz

    def on_device(queries, key_vectors, value_rows, cotangent):
        length, width = queries.shape
        factor = 1.0 / math.sqrt(DH * length * ctx)
        f32, bf16 = jnp.float32, jnp.bfloat16
        dma = pltpu.SemaphoreType.DMA
        vmem, hbm = pltpu.VMEM, pltpu.HBM
        ready = pl.pallas_call(
            functools.partial(kernel, nz, factor),
            out_shape=(vmem((length, width), bf16),) * 2
            + (vmem((length, width), f32),) * 4
            + (vmem((length, width), bf16),) * 4
            + (vmem((HEADS, 2, DH, DH), bf16),),
            in_specs=[pl.BlockSpec(memory_space=hbm)] * 4,
            out_specs=(pl.BlockSpec(memory_space=vmem),) * 11,
            scratch_shapes=[
                vmem((2, NX, DH, DH), f32),
                vmem((2, PIECES, 2 * NX, TALL, DH), f32),
                vmem((2, 2, NX, DH, DH), f32),
                vmem((2, PIECES, nz, 2, sub, DH), f32),
                vmem((2, PIECES, nz, 2, sub, DH), f32),
                vmem((2, PIECES, nz, 2, sub, DH), f32),
                vmem((2, PIECES, nz, 2, sub, DH), f32),
                vmem((2, PIECES, NX, TALL, DH), f32),
                dma((2, NX + 1)),
                dma((5,)),
                dma((2, PIECES)), dma((2, PIECES, 2)), dma((2, PIECES)), dma((2, PIECES)),
                pltpu.SemaphoreType.REGULAR,
            ],
            compiler_params=pltpu.CompilerParams(
                collective_id=0, has_side_effects=True, vmem_limit_bytes=32 * 1024 * 1024
            ),
            name="linear_attention",
        )(*(
            pltpu.with_memory_space_constraint(arr, hbm)
            for arr in (queries, key_vectors, value_rows, cotangent)
        ))
        out = jax.ShapeDtypeStruct((length, width), bf16)
        return pl.pallas_call(
            functools.partial(last_part, factor),
            out_shape=(out,) * 4,
            in_specs=[pl.BlockSpec(memory_space=vmem)] * 11,
            out_specs=(pl.BlockSpec(memory_space=hbm),) * 4,
            scratch_shapes=[
                vmem((length, width), bf16),
                vmem((length, width), bf16),
                dma((4,)),
            ],
            compiler_params=pltpu.CompilerParams(vmem_limit_bytes=16 * 1024 * 1024),
            name="last_part",
        )(*(pltpu.with_memory_space_constraint(arr, vmem) for arr in ready))

    spec = P(("grp", "ctx"), None)
    return jax.shard_map(
        on_device, mesh=mesh, in_specs=(spec,) * 4, out_specs=(spec,) * 4, check_vma=False
    )
```

```python
import functools
import math

import jax
import jax.numpy as jnp
from jax import lax
from jax.experimental import pallas as pl
from jax.experimental.pallas import tpu as pltpu
from jax.sharding import PartitionSpec as P

DH = 128
HEADS = 4
NX = 4
BLK = 256
PIECES = 2
FEW = 3
TALL = DH // PIECES
MESH = pl.DeviceIdType.MESH


def inner_first(left, right):
    return lax.dot_general(
        left, right, (((0,), (0,)), ((), ())), preferred_element_type=jnp.float32
    )


def inner_last(left, right):
    return lax.dot_general(
        left, right, (((1,), (1,)), ((), ())), preferred_element_type=jnp.float32
    )


def plain(left, right):
    return jnp.dot(left, right, preferred_element_type=jnp.float32)


def split(state):
    upper = state.astype(jnp.bfloat16)
    lower = (state - upper.astype(jnp.float32)).astype(jnp.bfloat16)
    return upper, lower


def inter_last(factor, out, acc, left, hi, lo, across, c, parts):
    both = jnp.concatenate([hi, lo], axis=1 if across else 0)
    for r in parts:
        own = pl.ds(r * BLK, BLK)
        lhs = left[own, c]
        lhs = jnp.concatenate([lhs, lhs], axis=1)
        inter = inner_last(lhs, both) if across else plain(lhs, both)
        out[own, c] = (factor * (acc[own, c] + inter)).astype(jnp.bfloat16)


def kernel(
    nz, factor,
    q_hbm, k_hbm, v_hbm, g_hbm,
    done_a, done_b, acc_a, acc_q, acc_k, acc_v, q, k, v, g, open_state,
    state, row_in, row_out, total, col_in, col_out, column, entering,
    in_sem, sent, got1, got2, got3, got4, ready,
):
    length = q.shape[0]
    blocks = length // BLK
    me = lax.axis_index("ctx")
    z = lax.div(me, NX)
    x = lax.rem(me, NX)
    grp = lax.axis_index("grp")
    core = lax.rem(grp, 2)
    scans = core == 1
    sub = TALL // nz

    def along_x(i):
        return lax.rem(x + i, NX)

    def along_z(i):
        return lax.rem(z + i, nz)

    def at(zz, xx, cc):
        return {"ctx": zz * NX + xx, "grp": grp - core + cc}

    def rows(part):
        return pl.ds(part * TALL, TALL)

    def cols(h):
        if isinstance(h, int):
            return pl.ds(h * DH, DH)
        return pl.ds(pl.multiple_of(h * DH, DH), DH)

    early = z < FEW

    ORDER = (1, 3, 2, 0)
    pairs = ((k_hbm, k), (v_hbm, v), (q_hbm, q), (g_hbm, g))

    def load_all(n):
        src, dst = pairs[n]
        return pltpu.make_async_copy(src, dst, in_sem.at[n % 2, NX])

    def load_head(n, i):
        src, dst = pairs[n]
        c = cols(along_x(i))
        return pltpu.make_async_copy(src.at[:, c], dst.at[:, c], in_sem.at[n % 2, i])

    def load(first, second):
        for i in ORDER:
            for n in first:
                load_head(n, i).start()
        for n in second:
            load_all(n).start()

    @pl.when(early)
    def _():
        load((0, 1), (2, 3))

    @pl.when(jnp.logical_not(early))
    def _():
        load((2, 3), (0, 1))

    barrier = pltpu.get_barrier_semaphore()

    @pl.when(scans)
    def _():
        for i in range(NX):
            pl.semaphore_signal(barrier, inc=1, device_id=at(z, along_x(i), 0), device_id_type=MESH)
        for i in range(1, nz):
            pl.semaphore_signal(barrier, inc=1, device_id=at(along_z(i), x, 1), device_id_type=MESH)

    @pl.when(jnp.logical_not(scans))
    def _():
        pl.semaphore_wait(barrier, NX)
        pl.semaphore_signal(ready, inc=1, device_id=at(z, x, 1), device_id_type=MESH)

    def send(src, dst, ssem, rsem, device):
        pltpu.make_async_remote_copy(
            src_ref=src, dst_ref=dst, send_sem=ssem, recv_sem=rsem,
            device_id=device, device_id_type=MESH,
        ).start()

    def arrived(ref, sem):
        pltpu.make_async_copy(ref, ref, sem).wait()

    def hand_in(st, part, i):
        send(
            state.at[st, i, rows(part)], row_in.at[st, part, core * NX + x],
            sent.at[0], got1.at[st, part], at(z, along_x(i), 1),
        )

    def hand_in_own(st, part):
        @pl.when(scans)
        def _():
            row_in[st, part, NX + x] = state[st, 0, rows(part)]

        @pl.when(jnp.logical_not(scans))
        def _():
            hand_in(st, part, 0)

    def states(st, first):
        left, right = ((k, v), (q, g))[st]
        if not first:
            load_all(2 * st).wait()
            load_all(2 * st + 1).wait()
        for i in ORDER:
            h = along_x(i)
            if first:
                load_head(2 * st, i).wait()
                load_head(2 * st + 1, i).wait()
            state[st, i] = inner_first(left[:, cols(h)], right[:, cols(h)])
            if first:
                if i == 1:
                    @pl.when(scans)
                    def _():
                        pl.semaphore_wait(ready, 1)
                hand_in(st, 0, i) if i > 0 else hand_in_own(st, 0)
        for part in range(1 if first else 0, PIECES):
            for i in ORDER[:3]:
                hand_in(st, part, i)
            hand_in_own(st, part)

    def row_scan(st, part, meet=False):
        arrived(row_in.at[st, part, pl.ds(0, 2 * NX - 1)], got1.at[st, part])
        order = list(range(NX)) if st == 0 else list(reversed(range(NX)))
        for cc in range(2):
            run = None
            for at_x in order:
                row_out[cc, st, at_x, rows(part)] = (
                    jnp.zeros((TALL, DH), jnp.float32) if run is None else run
                )
                new = row_in[st, part, cc * NX + at_x]
                run = new if run is None else run + new
            total[st, part, :, cc] = run.reshape(nz, sub, DH)
        if meet:
            pl.semaphore_wait(barrier, nz - 1)
        for i in range(1, nz):
            send(
                total.at[st, part, along_z(i)], col_in.at[st, part, z],
                sent.at[1], got2.at[st, part, jnp.where(early, 0, 1)], at(along_z(i), x, 1),
            )
        col_in[st, part, z] = total[st, part, z]

    def heard(st, part, few):
        group = got2.at[st, part, 0 if few else 1]
        among = FEW if few else nz - FEW
        inside = early if few else jnp.logical_not(early)

        @pl.when(inside)
        def _():
            arrived(col_in.at[st, part, pl.ds(0, among - 1)], group)

        @pl.when(jnp.logical_not(inside))
        def _():
            arrived(col_in.at[st, part, pl.ds(0, among)], group)

    def tell(st, part, dst):
        @pl.when(z != dst)
        def _():
            send(
                col_out.at[st, part, dst], column.at[st, part, z],
                sent.at[2], got3.at[st, part], at(dst, x, 1),
            )

    def col_scan(part):
        heard(1, part, True)
        heard(1, part, False)
        run = jnp.zeros((2, sub, DH), jnp.float32)
        for at_z in reversed(range(nz)):
            col_out[1, part, at_z] = run
            run = run + col_in[1, part, at_z]
        for at_z in range(nz):
            tell(1, part, at_z)
        column[1, part, z] = col_out[1, part, z]

    def col_scan_few(part):
        heard(0, part, True)
        run = jnp.zeros((2, sub, DH), jnp.float32)
        for at_z in range(FEW):
            run = run + col_in[0, part, at_z]
            col_out[0, part, at_z + 1] = run
        for at_z in range(1, FEW + 1):
            tell(0, part, at_z)

    def col_scan_rest(part):
        heard(0, part, False)
        run = col_out[0, part, FEW]
        for at_z in range(FEW, nz - 1):
            run = run + col_in[0, part, at_z]
            col_out[0, part, at_z + 1] = run
        for at_z in range(FEW + 1, nz):
            tell(0, part, at_z)

    def give_back(st, part, alone=False):
        if not alone:
            if st == 0:
                column[0, part, z] = col_out[0, part, z]
            arrived(column.at[st, part, pl.ds(0, nz - 1)], got3.at[st, part])
        for cc in range(2):
            if not alone:
                base = column[st, part, :, cc].reshape(TALL, DH)
            for i in (2, 1, 3, 0):
                here = row_out.at[cc, st, along_x(i), rows(part)]
                if not alone:
                    here[...] += base
                if cc == 0 or i > 0:
                    send(
                        here, entering.at[st, part, x],
                        sent.at[3 + cc], got4.at[st, part], at(z, along_x(i), cc),
                    )
        entering[st, part, x] = row_out[1, st, x, rows(part)]

    def give_first(part):
        @pl.when(z == 0)
        def _():
            give_back(0, part, True)

    def give_few(part):
        @pl.when(jnp.logical_and(z > 0, z <= FEW))
        def _():
            give_back(0, part)

    def give_rest(part):
        @pl.when(z > FEW)
        def _():
            give_back(0, part)

    def take(st, part):
        @pl.when(scans)
        def _():
            arrived(entering.at[st, part, pl.ds(0, NX - 1)], got4.at[st, part])

        @pl.when(jnp.logical_not(scans))
        def _():
            arrived(entering.at[st, part], got4.at[st, part])

    def entered(st, h):
        return jnp.concatenate([entering[st, part, h] for part in range(PIECES)], axis=0)

    causal = lax.broadcasted_iota(jnp.int32, (BLK, BLK), 0) >= lax.broadcasted_iota(
        jnp.int32, (BLK, BLK), 1
    )

    def unit(h, r):
        c = cols(h)
        own = pl.ds(r * BLK, BLK)
        q_r, g_r = q[own, c], g[own, c]
        until = (r + 1) * BLK

        def lower(left, right):
            parts = []
            for b in range(r + 1):
                w = inner_last(left, right[pl.ds(b * BLK, BLK), c])
                if b == r:
                    w = jnp.where(causal, w, 0.0)
                parts.append(w.astype(jnp.bfloat16))
            return parts[0] if r == 0 else jnp.concatenate(parts, axis=1)

        weights = lower(q_r, k)
        back = lower(g_r, v)
        acc_a[own, c] = plain(weights, v[:until, c])
        acc_q[own, c] = plain(back, k[:until, c])
        for acc, left, right in ((acc_k, back, q_r), (acc_v, weights, g_r)):
            add = inner_first(left, right)
            if r > 0:
                done = r * BLK
                acc[:done, c] += add[:done]
                acc[own, c] = add[done:]
            else:
                acc[own, c] = add

    def finish(st, h):
        c = cols(h)
        hi, lo = split(entered(st, h))
        accs = ((acc_a, acc_q), (acc_v, acc_k))[st]
        lefts = ((q, g), (k, v))[st]
        for out, acc, left, across in zip((done_a, done_b), accs, lefts, (False, True)):
            inter_last(factor, out, acc, left, hi, lo, across, c, range(blocks))

    def leave(st):
        for h in range(HEADS):
            open_state[h, 0], open_state[h, 1] = split(entered(st, h))

    @pl.when(early)
    def _():
        states(0, True)
        states(1, False)

    @pl.when(jnp.logical_not(early))
    def _():
        states(1, True)
        states(0, False)

    def first_scans():
        @pl.when(early)
        def _():
            for part in range(PIECES):
                row_scan(0, part, part == 0)

        @pl.when(jnp.logical_not(early))
        def _():
            for part in range(PIECES):
                row_scan(1, part, part == 0)

    def second_scans():
        @pl.when(early)
        def _():
            for part in range(PIECES):
                row_scan(1, part)
            for part in range(PIECES):
                give_first(part)
            for part in range(PIECES):
                col_scan_few(part)

        @pl.when(jnp.logical_not(early))
        def _():
            for part in range(PIECES):
                col_scan_few(part)
            for part in range(PIECES):
                row_scan(0, part)

    def third_scans():
        @pl.when(early)
        def _():
            for part in range(PIECES):
                give_back(1, part)
                col_scan_rest(part)

        @pl.when(jnp.logical_not(early))
        def _():
            for part in range(PIECES):
                col_scan_rest(part)
            for part in range(PIECES):
                give_back(1, part)

    units = [(h, r) for h in range(HEADS) for r in range(blocks)]
    steps = [
        6, (first_scans,), (second_scans,), (col_scan, 0), (col_scan, 1), (give_few, 0), (give_few, 1), 5,
        (third_scans,), (give_rest, 0), (give_rest, 1), 16,
    ]
    for step in steps:
        if isinstance(step, int):
            for _ in range(step):
                if units:
                    unit(*units.pop(0))
        else:
            pl.when(scans)(functools.partial(*step))
    for near, order in ((z <= FEW, (0, 1)), (z > FEW, (1, 0))):
        @pl.when(near)
        def _():
            for part in range(PIECES):
                take(order[0], part)
            for h in range(HEADS):
                finish(order[0], h)
            for part in range(PIECES):
                take(order[1], part)
            leave(order[1])

    def gone(ref, n):
        pltpu.make_async_copy(ref, ref, sent.at[n]).wait()

    @pl.when(scans)
    def _():
        gone(state.at[:, pl.ds(0, NX - 1)], 0)
        gone(total.at[:, :, pl.ds(0, nz - 1)], 1)
        gone(col_out.at[1, :, pl.ds(0, nz - 1)], 2)
        gone(col_out.at[0, :, pl.ds(0, nz - 2)], 2)

        @pl.when(z == 0)
        def _():
            gone(col_out.at[0, :, nz - 1], 2)

        gone(row_out.at[0], 3)
        gone(row_out.at[1, :, pl.ds(0, NX - 1)], 4)

    @pl.when(jnp.logical_not(scans))
    def _():
        gone(state, 0)


def last_part(
    factor,
    done_a, done_b, acc_a, acc_q, acc_k, acc_v, q, k, v, g, open_state,
    att_hbm, gq_hbm, gk_hbm, gv_hbm,
    late_a, late_b, sem,
):
    blocks = k.shape[0] // BLK
    z = lax.div(lax.axis_index("ctx"), NX)

    def write(n, src, dst, r):
        part = pl.ds(r * BLK, BLK)
        return pltpu.make_async_copy(src.at[part], dst.at[part], sem.at[n])

    def rest(first, second, accs, lefts):
        copies = []
        for r in range(blocks):
            copies.append(write(0, done_a, first[0], r))
            copies.append(write(1, done_b, first[1], r))
        for copy in copies:
            copy.start()
        for r in range(blocks):
            for h in range(HEADS):
                c = pl.ds(h * DH, DH)
                hi, lo = open_state[h, 0], open_state[h, 1]
                for out, acc, left, across in zip((late_a, late_b), accs, lefts, (False, True)):
                    inter_last(factor, out, acc, left, hi, lo, across, c, (r,))
            for n, src in ((2, late_a), (3, late_b)):
                copy = write(n, src, second[n - 2], r)
                copy.start()
                copies.append(copy)
        for n, src in enumerate((done_a, done_b, late_a, late_b)):
            pltpu.make_async_copy(src, src, sem.at[n]).wait()

    @pl.when(z <= FEW)
    def _():
        rest((att_hbm, gq_hbm), (gv_hbm, gk_hbm), (acc_v, acc_k), (k, v))

    @pl.when(z > FEW)
    def _():
        rest((gv_hbm, gk_hbm), (att_hbm, gq_hbm), (acc_a, acc_q), (q, g))


def solution(mesh):
    ctx = mesh.shape["ctx"]
    nz = ctx // NX
    sub = TALL // nz

    def on_device(queries, key_vectors, value_rows, cotangent):
        length, width = queries.shape
        factor = 1.0 / math.sqrt(DH * length * ctx)
        f32, bf16 = jnp.float32, jnp.bfloat16
        dma = pltpu.SemaphoreType.DMA
        vmem, hbm = pltpu.VMEM, pltpu.HBM
        ready = pl.pallas_call(
            functools.partial(kernel, nz, factor),
            out_shape=(vmem((length, width), bf16),) * 2
            + (vmem((length, width), f32),) * 4
            + (vmem((length, width), bf16),) * 4
            + (vmem((HEADS, 2, DH, DH), bf16),),
            in_specs=[pl.BlockSpec(memory_space=hbm)] * 4,
            out_specs=(pl.BlockSpec(memory_space=vmem),) * 11,
            scratch_shapes=[
                vmem((2, NX, DH, DH), f32),
                vmem((2, PIECES, 2 * NX, TALL, DH), f32),
                vmem((2, 2, NX, DH, DH), f32),
                vmem((2, PIECES, nz, 2, sub, DH), f32),
                vmem((2, PIECES, nz, 2, sub, DH), f32),
                vmem((2, PIECES, nz, 2, sub, DH), f32),
                vmem((2, PIECES, nz, 2, sub, DH), f32),
                vmem((2, PIECES, NX, TALL, DH), f32),
                dma((2, NX + 1)),
                dma((5,)),
                dma((2, PIECES)), dma((2, PIECES, 2)), dma((2, PIECES)), dma((2, PIECES)),
                pltpu.SemaphoreType.REGULAR,
            ],
            compiler_params=pltpu.CompilerParams(
                collective_id=0, has_side_effects=True, vmem_limit_bytes=32 * 1024 * 1024
            ),
            name="linear_attention",
        )(*(
            pltpu.with_memory_space_constraint(arr, hbm)
            for arr in (queries, key_vectors, value_rows, cotangent)
        ))
        out = jax.ShapeDtypeStruct((length, width), bf16)
        return pl.pallas_call(
            functools.partial(last_part, factor),
            out_shape=(out,) * 4,
            in_specs=[pl.BlockSpec(memory_space=vmem)] * 11,
            out_specs=(pl.BlockSpec(memory_space=hbm),) * 4,
            scratch_shapes=[
                vmem((length, width), bf16),
                vmem((length, width), bf16),
                dma((4,)),
            ],
            compiler_params=pltpu.CompilerParams(vmem_limit_bytes=16 * 1024 * 1024),
            name="last_part",
        )(*(pltpu.with_memory_space_constraint(arr, vmem) for arr in ready))

    spec = P(("grp", "ctx"), None)
    return jax.shard_map(
        on_device, mesh=mesh, in_specs=(spec,) * 4, out_specs=(spec,) * 4, check_vma=False
    )
```
